32 devices in a mesh: streams: 2 (over y), span: 4 (over z), head: 2 (over x), seq: 2 (over core).
Axes of the slice: x: 2, y: 2, z: 4, core: 2. Of those that a mesh axis runs over, the one named last changes fastest.
Arguments:
- query_rows: bfloat16 [4096, 1280], P(('streams', 'span', 'seq'), 'head'), parts along dimension 0, may hold values from -100 to 100
- key_rows: bfloat16 [4096, 1280], P(('streams', 'span', 'seq'), 'head'), parts along dimension 0, may hold values from -5 to 5
- value_rows: bfloat16 [4096, 1280], P(('streams', 'span', 'seq'), 'head'), parts along dimension 0, may hold values from -6 to 6
- out_weight: bfloat16 [1280, 5120], P('head', 'seq'), may hold values from -0.59765625 to 0.59765625
- gate_table: float32 [4, 5120], P(None, 'head'), may hold values from 0.5 to 2
- step_index: int32 [8], P('streams'), parts along dimension 0, may hold values from 0 to 3
- block_mask: int32 [8, 4], P('streams'), parts along dimension 0, may hold values from 0 to 1, as said below
Outputs:
- gated_update: bfloat16 [4096, 5120], P(('streams', 'span', 'seq'), 'head'), parts along dimension 0
The draws below stay inside these ranges and needn't reach their ends.
There are 2 independent parts, one for each index of `streams`. The reference program is written for one: setup_inputs(seed, part) draws one part's arguments, and reference() takes and returns one part's arrays. A program takes and returns all parts, laid end to end along the dimension named above; an argument that names none is the same for every part. Nothing has to cross between parts.
Inputs may be any that keep to these rules, and one draw needn't show every extreme that they name: block_mask[c, c] = 1 and block_mask[c, e] = 0 for e > c; entries below the diagonal are 0 or 1.
All inputs are finite; a program needn't handle non-finite values.
Results may differ from the reference program's by a relative error of at most 0.017.
Values may be sent and summed in bfloat16 or wider, within the bound.
No kernel may reach another device: no remote copies, remote signals or barrier semaphores. Data moves between devices by JAX's collectives and lax.ppermute only.
A program may use at most 192 MiB of HBM per device.

```python
import math
import jax
import jax.numpy as jnp
from jax import lax

D = 5120
HD = 128
TOK_DEV = 256
STEPS = 4
HEADS = 10
SPANS = 4
TOKENS = 2048
N_SPAN = 4
N_SEQ = 2


def paired_draw(key):
    base = jax.random.fold_in(key, 7701)
    key_vals = jax.random.normal(jax.random.fold_in(base, 1), (TOKENS, HEADS * HD), jnp.float32)
    key_vals = jnp.clip(key_vals, -5.0, 5.0)
    query_vals = 1.5 * jax.random.normal(jax.random.fold_in(base, 2), (TOKENS, HEADS * HD), jnp.float32)
    query_vals = jnp.clip(query_vals, -8.0, 8.0)
    return (query_vals, key_vals)


def draw_query_rows(key, part):
    return paired_draw(key)[0].astype(jnp.bfloat16)


def draw_key_rows(key, part):
    return paired_draw(key)[1].astype(jnp.bfloat16)


def draw_block_mask(key, part):
    bits = jax.random.randint(jax.random.fold_in(key, 4411), (SPANS, SPANS), 0, 4)
    rows = jnp.arange(SPANS, dtype=jnp.int32)[:, None]
    cols = jnp.arange(SPANS, dtype=jnp.int32)[None, :]
    lower = jnp.where(rows > cols, jnp.where(bits > 0, 1, 0), 0)
    return (lower + jnp.where(rows == cols, 1, 0)).astype(jnp.int32)


def set_ends(drawn, key, smallest, largest):
    longest = drawn.shape.index(max(drawn.shape))
    spots = []
    for shift in (0, 1):
        where = [jax.random.randint(jax.random.fold_in(key, axis), (), 0, length) for axis, length in enumerate(drawn.shape)]
        where[longest] = (where[longest] + shift) % drawn.shape[longest]
        spots.append(tuple(where))
    return drawn.at[spots[0]].set(smallest).at[spots[1]].set(largest)


def shard_levels(own_key, shape, split, low, high):
    gain, own = 1.0, jax.random.fold_in(own_key, 6)
    for axis_at, parts in split:
        steps = jnp.exp(jax.random.uniform(jax.random.fold_in(own, axis_at), (parts,), jnp.float32, low / len(split), high / len(split)))
        gain = gain * jnp.repeat(steps, shape[axis_at] // parts).reshape([-1 if axis == axis_at else 1 for axis in range(len(shape))])
    return gain


def noise(own_key, dims, deviation, reach, cuts=(), kind=jnp.bfloat16):
    level = shard_levels(own_key, dims, cuts, -0.22, 0.18) if cuts else 1.0
    values = jax.random.normal(own_key, dims, jnp.float32) * deviation * level
    return jnp.minimum(jnp.maximum(values, -reach), reach).astype(kind)


def setup_inputs(seed: int = 0, part: int = 0) -> dict:
    keys = jax.random.split(jax.random.key(seed), 8)
    own_keys = jax.random.split(jax.random.fold_in(keys[7], part), 8)
    query_rows = draw_query_rows(jax.random.fold_in(jax.random.fold_in(keys[7], part), 71), part)
    key_rows = draw_key_rows(jax.random.fold_in(jax.random.fold_in(keys[7], part), 71), part)
    value_rows = noise(own_keys[2], (TOKENS, HEADS * HD), 1.0, 6.0, ((0, 8), (1, 2)))
    out_weight = noise(keys[3], (HEADS * HD, D), 0.1, 0.59765625, ((0, 2), (1, 2)))
    gate_table = jnp.clip(0.5 + 1.5 * jax.random.uniform(keys[4], (STEPS, D), jnp.float32) ** shard_levels(keys[4], (STEPS, D), ((1, 2),), -0.2, 0.2), 0.5, 2.0)
    step_index = set_ends(jax.random.randint(own_keys[5], (SPANS,), 0, STEPS), jax.random.fold_in(own_keys[5], 1), 0, STEPS - 1).astype(jnp.int32)
    block_mask = draw_block_mask(jax.random.fold_in(jax.random.fold_in(keys[7], part), 71), part)
    return dict(query_rows=query_rows, key_rows=key_rows, value_rows=value_rows, out_weight=out_weight, gate_table=gate_table, step_index=step_index, block_mask=block_mask)


def reference(query_rows, key_rows, value_rows, out_weight, gate_table, step_index, block_mask):
    span_tok = TOK_DEV * N_SEQ
    span_count = N_SPAN
    head_count = query_rows.shape[1] // HD
    query_blocks = query_rows.reshape(span_count, span_tok, head_count, HD)
    key_all = key_rows.reshape(-1, head_count, HD).astype(jnp.float32)
    value_all = value_rows.reshape(-1, head_count, HD).astype(jnp.float32)
    key_group = (jnp.arange(key_all.shape[0], dtype=jnp.int32) // span_tok).astype(jnp.int32)

    def one_span(packed):
        query_block, group = packed
        visible = block_mask[group][key_group] == 1
        scores = jnp.einsum('thd,khd->htk', query_block.astype(jnp.float32), key_all) / math.sqrt(HD)
        scores = jnp.where(visible[None, None, :], scores, -jnp.inf)
        top_score = lax.optimization_barrier(jnp.max(scores, axis=2, keepdims=True))
        probs = jnp.where(visible[None, None, :], jnp.exp(scores - top_score), 0.0)
        denom = lax.optimization_barrier(jnp.sum(probs, axis=2))
        probs_low = probs.astype(jnp.bfloat16).astype(jnp.float32)
        summed = jnp.einsum('htk,khd->htd', probs_low, value_all) / denom[:, :, None]
        attended = jnp.transpose(summed, (1, 0, 2)).reshape(span_tok, head_count * HD).astype(jnp.bfloat16)
        projected = jnp.dot(attended, out_weight, preferred_element_type=jnp.float32)
        gate_row = gate_table[step_index[group]]
        return (gate_row[None, :] * projected).astype(jnp.bfloat16)
    outputs = lax.map(one_span, (query_blocks, jnp.arange(span_count, dtype=jnp.int32)))
    return outputs.reshape(span_count * span_tok, -1)
```

```python
import functools
import math

import jax
import jax.numpy as jnp
from jax import lax
from jax.experimental import pallas as pl
from jax.experimental.pallas import tpu as pltpu
from jax.sharding import PartitionSpec as P

HD = 128
NEG = -1e30
STAT = 16
VMEM_LIMIT = 16 * 1024 * 1024


def dot(a, b, dims):
    return lax.dot_general(a, b, (dims, ((), ())), preferred_element_type=jnp.float32)


def parts_of(x):
    hi = x.astype(jnp.bfloat16)
    rest = x - hi.astype(jnp.float32)
    mid = rest.astype(jnp.bfloat16)
    low = (rest - mid.astype(jnp.float32)).astype(jnp.bfloat16)
    return hi, mid, low


def write_message(acc, top, out_ref):
    rows = acc.shape[0]
    total = acc[:, HD:]
    live = total > 0.0
    safe = jnp.where(live, total, 1.0)
    out_ref[0:rows, :] = (acc[:, :HD] / safe).astype(jnp.bfloat16)
    lse = jnp.where(live, top + jnp.log2(safe), NEG)
    hi, mid, low = parts_of(lse)
    lane = lax.broadcasted_iota(jnp.int32, lse.shape, 1)
    zero = jnp.zeros_like(hi)
    packed = jnp.where(lane == 0, hi, jnp.where(lane == 1, mid, jnp.where(lane == 2, low, zero)))
    row = lax.broadcasted_iota(jnp.int32, (STAT, HD), 0)
    col = lax.broadcasted_iota(jnp.int32, (STAT, HD), 1)
    stats = jnp.zeros((STAT, HD), jnp.float32)
    for block in range(rows // HD):
        pick = jnp.where((row - 3 * block == col) & (col < 3), 1.0, 0.0).astype(jnp.bfloat16)
        stats += dot(pick, packed[block * HD : (block + 1) * HD], ((1,), (1,)))
    out_ref[rows:, :] = stats.astype(jnp.bfloat16)


def read_message(msg_ref, rows):
    row = lax.broadcasted_iota(jnp.int32, (STAT, HD), 0)
    blocks = []
    for block in range(rows // HD):
        pick = jnp.where((row >= 3 * block) & (row < 3 * block + 3), 1.0, 0.0).astype(jnp.bfloat16)
        blocks.append(dot(msg_ref[rows:, :], pick, ((0,), (0,))))
    return msg_ref[0:rows, :].astype(jnp.float32), jnp.concatenate(blocks, axis=0)


def attend_kernel(first, emit, slot, meta_ref, *refs):
    q_ref, ka_ref, va_ref, kb_ref, vb_ref = refs[:5]
    refs = refs[5:]
    rows = q_ref.shape[0]
    if not first:
        acc_in, top_in = refs[:2]
        refs = refs[2:]
    visible = meta_ref[slot] == 1

    def store(acc, top):
        if emit:
            write_message(acc, top, refs[0])
        else:
            refs[0][...] = acc
            refs[1][...] = top

    @pl.when(visible)
    def _():
        scale = math.log2(math.e) / math.sqrt(HD)
        q = q_ref[...]
        score_a = dot(q, ka_ref[...], ((1,), (1,)))
        score_b = dot(q, kb_ref[...], ((1,), (1,)))
        high = jnp.maximum(
            jnp.max(score_a, axis=1, keepdims=True), jnp.max(score_b, axis=1, keepdims=True)
        )
        high = jnp.broadcast_to(high * scale, (rows, HD))
        top = high if first else jnp.maximum(top_in[...], high)
        line = top[:, :1]
        prob_a = jnp.exp2(score_a * scale - line).astype(jnp.bfloat16)
        prob_b = jnp.exp2(score_b * scale - line).astype(jnp.bfloat16)
        ones = jnp.ones((ka_ref.shape[0], HD), jnp.bfloat16)
        acc = dot(prob_a, jnp.concatenate([va_ref[...], ones], axis=1), ((1,), (0,)))
        acc += dot(prob_b, jnp.concatenate([vb_ref[...], ones], axis=1), ((1,), (0,)))
        if not first:
            fade = jnp.exp2(top_in[...] - top)
            acc += acc_in[...] * jnp.concatenate([fade, fade], axis=1)
        store(acc, top)

    @pl.when(jnp.logical_not(visible))
    def _():
        if first:
            store(jnp.zeros((rows, 2 * HD), jnp.float32), jnp.full((rows, HD), NEG, jnp.float32))
        else:
            store(acc_in[...], top_in[...])


def attend(meta, slot, q, head_at, kv, kv_other, state, emit=False):
    rows, keys = q.shape[0], kv.shape[0]
    heads = kv.shape[1] // (2 * HD)
    first = state is None
    kv_specs = [
        pl.BlockSpec((keys, HD), lambda h, m: (0, h)),
        pl.BlockSpec((keys, HD), lambda h, m: (0, heads + h)),
    ]
    state_specs = [
        pl.BlockSpec((rows, 2 * HD), lambda h, m: (0, h)),
        pl.BlockSpec((rows, HD), lambda h, m: (0, h)),
    ]
    state_shape = [
        jax.ShapeDtypeStruct((rows, heads * 2 * HD), jnp.float32),
        jax.ShapeDtypeStruct((rows, heads * HD), jnp.float32),
    ]
    out_specs, out_shape = state_specs, state_shape
    if emit:
        out_specs = [pl.BlockSpec((rows + STAT, HD), lambda h, m: (0, h))]
        out_shape = [jax.ShapeDtypeStruct((rows + STAT, heads * HD), jnp.bfloat16)]
    in_specs = [pl.BlockSpec((rows, HD), lambda h, m: (0, head_at + h))] + kv_specs * 2
    operands = [q, kv, kv, kv_other, kv_other]
    if not first:
        in_specs += state_specs
        operands += list(state)
    out = pl.pallas_call(
        functools.partial(attend_kernel, first, emit, slot),
        out_shape=out_shape,
        grid_spec=pltpu.PrefetchScalarGridSpec(
            num_scalar_prefetch=1, grid=(heads,), in_specs=in_specs, out_specs=out_specs
        ),
        compiler_params=pltpu.CompilerParams(vmem_limit_bytes=VMEM_LIMIT),
        cost_estimate=pl.CostEstimate(flops=1, transcendentals=0, bytes_accessed=1),
        name="attend",
    )(meta, *operands)
    return out[0] if emit else tuple(out)


def finish_kernel(slot, meta_ref, acc_ref, top_ref, msg_ref, out_ref):
    rows = acc_ref.shape[0]
    helped = meta_ref[slot] == 1

    @pl.when(helped)
    def _():
        part, lse = read_message(msg_ref, rows)
        high = jnp.maximum(top_ref[...], lse)
        mine, theirs = jnp.exp2(top_ref[...] - high), jnp.exp2(lse - high)
        total = acc_ref[:, HD:] * mine + theirs
        out_ref[...] = ((acc_ref[:, :HD] * mine + part * theirs) / total).astype(jnp.bfloat16)

    @pl.when(jnp.logical_not(helped))
    def _():
        out_ref[...] = (acc_ref[:, :HD] / acc_ref[:, HD:]).astype(jnp.bfloat16)


def finish(meta, slot, state, message):
    acc, top = state
    rows, heads = acc.shape[0], top.shape[1] // HD
    return pl.pallas_call(
        functools.partial(finish_kernel, slot),
        out_shape=jax.ShapeDtypeStruct((rows, heads * HD), jnp.bfloat16),
        grid_spec=pltpu.PrefetchScalarGridSpec(
            num_scalar_prefetch=1,
            grid=(heads,),
            in_specs=[
                pl.BlockSpec((rows, 2 * HD), lambda h, m: (0, h)),
                pl.BlockSpec((rows, HD), lambda h, m: (0, h)),
                pl.BlockSpec((rows + STAT, HD), lambda h, m: (0, h)),
            ],
            out_specs=pl.BlockSpec((rows, HD), lambda h, m: (0, h)),
        ),
        compiler_params=pltpu.CompilerParams(vmem_limit_bytes=VMEM_LIMIT),
        cost_estimate=pl.CostEstimate(flops=1, transcendentals=0, bytes_accessed=1),
        name="finish",
    )(meta, acc, top, message)


def project_kernel(groups, slots, meta_ref, *refs):
    mine, theirs = refs[:groups], refs[groups : 2 * groups]
    w_near, w_far, gate_ref, out_ref = refs[2 * groups :]
    straight = meta_ref[slots[0]] == 1
    total, at = None, 0
    for own_ref, far_ref in zip(mine, theirs):
        own, far = own_ref[...], far_ref[...]
        width = own.shape[1]
        near = jnp.where(straight, own, far)
        other = jnp.where(straight, far, own)
        term = dot(near, w_near[at : at + width, :], ((1,), (0,)))
        term += dot(other, w_far[at : at + width, :], ((1,), (0,)))
        total = term if total is None else total + term
        at += width
    gate = gate_ref[pl.ds(meta_ref[slots[1]], 1), :]
    out_ref[...] = (gate * total).astype(jnp.bfloat16)


def project(meta, slots, mine, theirs, w_near, w_far, gate_table):
    rows, depth, columns = mine[0].shape[0], w_near.shape[0], w_near.shape[1]
    tile = 512
    whole = [pl.BlockSpec(x.shape, lambda c, m: (0, 0)) for x in mine + theirs]
    return pl.pallas_call(
        functools.partial(project_kernel, len(mine), slots),
        out_shape=jax.ShapeDtypeStruct((rows, columns), jnp.bfloat16),
        grid_spec=pltpu.PrefetchScalarGridSpec(
            num_scalar_prefetch=1,
            grid=(columns // tile,),
            in_specs=whole
            + [
                pl.BlockSpec((depth, tile), lambda c, m: (0, c)),
                pl.BlockSpec((depth, tile), lambda c, m: (0, c)),
                pl.BlockSpec((gate_table.shape[0], tile), lambda c, m: (0, c)),
            ],
            out_specs=pl.BlockSpec((rows, tile), lambda c, m: (0, c)),
        ),
        compiler_params=pltpu.CompilerParams(vmem_limit_bytes=VMEM_LIMIT),
        cost_estimate=pl.CostEstimate(flops=1, transcendentals=0, bytes_accessed=1),
        name="project",
    )(meta, *mine, *theirs, w_near, w_far, gate_table)


def after(value, done):
    return lax.optimization_barrier((value, done))[0]


def swap_pairs(count):
    return [(i, count - 1 - i) for i in range(count)]


def on_device(query_rows, key_rows, value_rows, out_weight, gate_table, step_index, block_mask):
    heads = query_rows.shape[1] // HD
    spans, cores, sides = lax.axis_size("span"), lax.axis_size("seq"), lax.axis_size("head")
    span, core, side = lax.axis_index("span"), lax.axis_index("seq"), lax.axis_index("head")
    helper = span == spans - 2
    ids = jnp.arange(spans, dtype=jnp.int32)

    back = span - ids
    holds = back[:, None] == ids[None, :]
    own_row = jnp.sum(jnp.where((ids == span)[:, None], block_mask, 0), axis=0)
    sees = jnp.sum(jnp.where(holds, own_row[None, :], 0), axis=1)
    sees = jnp.where((ids == 0) | (span != spans - 1), sees, 0)
    help_row = jnp.where(helper, block_mask[spans - 1], 0)
    helps = jnp.sum(jnp.where(holds, help_row[None, :], 0), axis=1)
    my_step = jnp.sum(jnp.where(ids == span, step_index, 0))
    tail = jnp.stack([(span == spans - 1).astype(jnp.int32), (side == core).astype(jnp.int32), my_step])
    meta = jnp.concatenate([sees, helps, tail]).astype(jnp.int32)
    at_helped, at_straight, at_step = 2 * spans, 2 * spans + 1, 2 * spans + 2

    cuts = [0, (heads + 1) // 2, heads]
    groups = [(cuts[i], cuts[i + 1]) for i in range(2)]
    held = [
        jnp.concatenate([key_rows[:, a * HD : b * HD], value_rows[:, a * HD : b * HD]], axis=1)
        for a, b in groups
    ]
    asked = lax.ppermute(query_rows, "span", [(spans - 1, spans - 2)])
    if sides == cores:
        turn = [(a * cores + b, b * sides + a) for a in range(sides) for b in range(cores)]
        w_near = lax.ppermute(out_weight, ("head", "seq"), turn)

    own, lent = [None] * 2, [None] * 2
    done = ()
    for step in range(spans - 1):
        for g, (a, b) in enumerate(groups):
            if step:
                hops = [(i, i + 1) for i in range(step - 1, spans - 2)]
                held[g] = after(lax.ppermute(held[g], "span", hops), done)
            across = lax.ppermute(held[g], "seq", swap_pairs(cores))
            last = step == spans - 2
            lent[g] = attend(meta, spans + step, asked, a, held[g], across, lent[g], emit=last)
            mine = after(query_rows, lent[g]) if step else query_rows
            own[g] = attend(meta, step, mine, a, held[g], across, own[g])
            if step or g:
                done = (lent[g], own[g]) if step else (lent, own)
    back_up = [(spans - 2, spans - 1)]
    message = [lax.ppermute(x, "span", back_up) for x in lent]
    message[0] = after(message[0], own[1])
    mine = [finish(meta, at_helped, own[g], message[g]) for g in range(2)]

    if sides == cores == 2:
        theirs = [lax.ppermute(x, "head", swap_pairs(sides)) for x in mine]
        w_near = after(w_near, mine[0])
        w_far = lax.ppermute(w_near, "seq", swap_pairs(cores))
        return project(meta, (at_straight, at_step), mine, theirs, w_near, w_far, gate_table)
    weight = lax.all_gather(out_weight, "seq", axis=1, tiled=True)
    projected = jnp.dot(jnp.concatenate(mine, axis=1), weight, preferred_element_type=jnp.float32)
    shared = lax.psum_scatter(projected.astype(jnp.bfloat16), "head", scatter_dimension=1, tiled=True)
    step_ids = jnp.arange(gate_table.shape[0], dtype=jnp.int32)
    gate_row = jnp.sum(jnp.where((step_ids == my_step)[:, None], gate_table, 0.0), axis=0)
    return (gate_row[None, :] * shared.astype(jnp.float32)).astype(jnp.bfloat16)


def solution(mesh):
    in_specs = (
        P(("streams", "span", "seq"), "head"),
        P(("streams", "span", "seq"), "head"),
        P(("streams", "span", "seq"), "head"),
        P("head", "seq"),
        P(None, "head"),
        P("streams"),
        P("streams", None),
    )
    out_specs = P(("streams", "span", "seq"), "head")
    return jax.shard_map(
        on_device, mesh=mesh, in_specs=in_specs, out_specs=out_specs, check_vma=False
    )
```

```python
import functools
import math

import jax
import jax.numpy as jnp
from jax import lax
from jax.experimental import pallas as pl
from jax.experimental.pallas import tpu as pltpu
from jax.sharding import PartitionSpec as P

HD = 128
NEG = -1e30
STAT = 16
VMEM_LIMIT = 16 * 1024 * 1024
BRIEF = pl.CostEstimate(flops=1, transcendentals=0, bytes_accessed=1)


def dot(a, b, dims):
    return lax.dot_general(a, b, (dims, ((), ())), preferred_element_type=jnp.float32)


def parts_of(x):
    hi = x.astype(jnp.bfloat16)
    rest = x - hi.astype(jnp.float32)
    mid = rest.astype(jnp.bfloat16)
    low = (rest - mid.astype(jnp.float32)).astype(jnp.bfloat16)
    return hi, mid, low


def write_message(acc, top, out_ref, at):
    rows = acc.shape[0]
    lanes = slice(at, at + HD)
    total = acc[:, HD:]
    live = total > 0.0
    safe = jnp.where(live, total, 1.0)
    out_ref[0:rows, lanes] = (acc[:, :HD] / safe).astype(jnp.bfloat16)
    lse = jnp.where(live, top + jnp.log2(safe), NEG)
    hi, mid, low = parts_of(lse)
    lane = lax.broadcasted_iota(jnp.int32, lse.shape, 1)
    zero = jnp.zeros_like(hi)
    packed = jnp.where(lane == 0, hi, jnp.where(lane == 1, mid, jnp.where(lane == 2, low, zero)))
    row = lax.broadcasted_iota(jnp.int32, (STAT, HD), 0)
    col = lax.broadcasted_iota(jnp.int32, (STAT, HD), 1)
    stats = jnp.zeros((STAT, HD), jnp.float32)
    for block in range(rows // HD):
        pick = jnp.where((row - 3 * block == col) & (col < 3), 1.0, 0.0).astype(jnp.bfloat16)
        stats += dot(pick, packed[block * HD : (block + 1) * HD], ((1,), (1,)))
    out_ref[rows:, lanes] = stats.astype(jnp.bfloat16)


def read_message(msg_ref, rows, at):
    lanes = slice(at, at + HD)
    row = lax.broadcasted_iota(jnp.int32, (STAT, HD), 0)
    blocks = []
    for block in range(rows // HD):
        pick = jnp.where((row >= 3 * block) & (row < 3 * block + 3), 1.0, 0.0).astype(jnp.bfloat16)
        blocks.append(dot(msg_ref[rows:, lanes], pick, ((0,), (0,))))
    return msg_ref[0:rows, lanes].astype(jnp.float32), jnp.concatenate(blocks, axis=0)


def visible_of(role, step, mask_ref):
    span, spans = lax.axis_index("span"), mask_ref.shape[1]
    keys = jnp.maximum(span - step, 0)
    if role == "own":
        there = (span >= step) if step == 0 else (span >= step) & (span != spans - 1)
        return there & (mask_ref[span, keys] == 1)
    return (span == spans - 2) & (span >= step) & (mask_ref[spans - 1, keys] == 1)


def wide(h):
    return slice(2 * h * HD, 2 * (h + 1) * HD)


def attend_kernel(roles, step, span_of_heads, pieces, emit, mask_ref, *refs):
    low, high = span_of_heads
    first = step == 0
    k_ref, v_refs, refs = refs[0], refs[1 : 1 + pieces], refs[1 + pieces :]
    q_refs, refs = refs[: 2 * len(roles)], refs[2 * len(roles) :]
    if not first:
        refs = refs[2 * len(roles) :]
    rows = q_refs[0].shape[0]
    scale = math.log2(math.e) / math.sqrt(HD)

    def values_of(h):
        at = h - low
        for v_ref in v_refs:
            heads = v_ref.shape[1] // HD
            if at < heads:
                return v_ref[:, at * HD : (at + 1) * HD]
            at -= heads

    for i, role in enumerate(roles):
        acc_ref, top_ref = refs[2 * i : 2 * i + 2]
        visible = visible_of(role, step, mask_ref)

        @pl.when(visible)
        def _():
            ones = jnp.ones((k_ref.shape[0], HD), jnp.bfloat16)
            for h in range(low, high):
                lanes = slice(h * HD, (h + 1) * HD)
                k, v = k_ref[:, lanes], jnp.concatenate([values_of(h), ones], axis=1)
                for half in range(2):
                    at = slice(half * rows, (half + 1) * rows)
                    score = dot(q_refs[2 * i + half][:, lanes], k, ((1,), (1,)))
                    peak = jnp.max(score, axis=1, keepdims=True) * scale
                    peak = jnp.broadcast_to(peak, (rows, HD))
                    top = peak if first else jnp.maximum(top_ref[at, lanes], peak)
                    prob = jnp.exp2(score * scale - top[:, :1]).astype(jnp.bfloat16)
                    acc = dot(prob, v, ((1,), (0,)))
                    if not first:
                        fade = jnp.exp2(top_ref[at, lanes] - top)
                        acc += acc_ref[at, wide(h)] * jnp.concatenate([fade, fade], axis=1)
                    acc_ref[at, wide(h)] = acc
                    top_ref[at, lanes] = top

        if first:

            @pl.when(jnp.logical_not(visible))
            def _():
                acc_ref[...] = jnp.zeros(acc_ref.shape, jnp.float32)
                top_ref[...] = jnp.full(top_ref.shape, NEG, jnp.float32)

        if emit:
            def write():
                for h in range(low, high):
                    top = top_ref[rows:, h * HD : (h + 1) * HD]
                    write_message(acc_ref[rows:, wide(h)], top, refs[-1], (h - low) * HD)

            if role == "lent":
                pl.when(lax.axis_index("span") == mask_ref.shape[1] - 2)(write)
            else:
                write()


def attend(mask, roles, step, span_of_heads, key, values, queries, states, emit=False):
    rows, width = key.shape[0], key.shape[1]
    some = span_of_heads[1] - span_of_heads[0]
    state_shape = [
        jax.ShapeDtypeStruct((2 * rows, 2 * width), jnp.float32),
        jax.ShapeDtypeStruct((2 * rows, width), jnp.float32),
    ]
    out_shape = state_shape * len(roles)
    if emit:
        out_shape.append(jax.ShapeDtypeStruct((rows + STAT, some * HD), jnp.bfloat16))
    operands = [key, *values, *queries]
    aliases = {}
    if step:
        aliases = {1 + len(operands) + i: i for i in range(2 * len(roles))}
        for state in states:
            operands += list(state)
    out = pl.pallas_call(
        functools.partial(attend_kernel, roles, step, span_of_heads, len(values), emit),
        out_shape=out_shape,
        in_specs=[pl.BlockSpec(memory_space=pltpu.SMEM)]
        + [pl.BlockSpec(memory_space=pltpu.VMEM)] * len(operands),
        out_specs=[pl.BlockSpec(memory_space=pltpu.VMEM)] * len(out_shape),
        input_output_aliases=aliases,
        compiler_params=pltpu.CompilerParams(vmem_limit_bytes=VMEM_LIMIT),
        cost_estimate=BRIEF,
        name="attend_" + "_".join(roles) + str(step) + str(span_of_heads[0]),
    )(mask, *operands)
    states = [tuple(out[2 * i : 2 * i + 2]) for i in range(len(roles))]
    return (states, out[-1]) if emit else states


def join_kernel(span_of_heads, forward, mask_ref, acc_ref, top_ref, mate_ref, *refs):
    low, high = span_of_heads
    span, spans = lax.axis_index("span"), mask_ref.shape[1]
    out_ref = refs[-1]
    rows = mate_ref.shape[0] - STAT

    def run(messages):
        for h in range(low, high):
            at = (h - low) * HD
            acc, top = acc_ref[0:rows, wide(h)], top_ref[0:rows, h * HD : (h + 1) * HD]
            for ref, is_mate in messages:
                part, lse = read_message(ref, rows, h * HD if is_mate and not forward else at)
                peak = jnp.maximum(top, lse)
                mine, theirs = jnp.exp2(top - peak), jnp.exp2(lse - peak)
                theirs = jnp.where(lse > 0.5 * NEG, theirs, 0.0)
                acc = acc * jnp.concatenate([mine, mine], axis=1) + jnp.concatenate([part * theirs, theirs], axis=1)
                top = peak
            if forward:
                write_message(acc, top, out_ref, at)
            else:
                out_ref[:, at : at + HD] = (acc[:, :HD] / acc[:, HD:]).astype(jnp.bfloat16)

    if forward:
        pl.when(span == spans - 2)(lambda: run([(mate_ref, True)]))
    else:
        pl.when(span == spans - 1)(lambda: run([(mate_ref, True), (refs[0], False)]))
        pl.when(span != spans - 1)(lambda: run([(mate_ref, True)]))


def join(mask, span_of_heads, state, mate, message=None):
    forward = message is None
    rows, width = mate.shape[0] - STAT, (span_of_heads[1] - span_of_heads[0]) * HD
    operands = [*state, mate] + ([] if forward else [message])
    return pl.pallas_call(
        functools.partial(join_kernel, span_of_heads, forward),
        out_shape=jax.ShapeDtypeStruct((rows + STAT if forward else rows, width), jnp.bfloat16),
        in_specs=[pl.BlockSpec(memory_space=pltpu.SMEM)]
        + [pl.BlockSpec(memory_space=pltpu.VMEM)] * len(operands),
        out_specs=pl.BlockSpec(memory_space=pltpu.VMEM),
        compiler_params=pltpu.CompilerParams(vmem_limit_bytes=VMEM_LIMIT),
        cost_estimate=BRIEF,
        name=("forward" if forward else "join") + str(span_of_heads[0]),
    )(mask, *operands)


def project_kernel(groups, tile, step_ref, *refs):
    mine, theirs = refs[:groups], refs[groups : 2 * groups]
    w_own, w_mate, w_far, w_back, gate_ref, out_ref, stage, sems = refs[2 * groups :]
    straight = lax.axis_index("head") == lax.axis_index("seq")
    tiles = out_ref.shape[1] // tile
    gate_row = pl.ds(step_ref[lax.axis_index("span")], 1)

    def copy(t):
        return pltpu.make_async_copy(stage.at[t], out_ref.at[:, t * tile : (t + 1) * tile], sems.at[t])

    def run(w_mine, w_theirs):
        for t in range(tiles):
            lanes = slice(t * tile, (t + 1) * tile)
            total, at = None, 0
            for own_ref, far_ref in zip(mine, theirs):
                width = own_ref.shape[1]
                term = dot(own_ref[...], w_mine[at : at + width, lanes], ((1,), (0,)))
                term += dot(far_ref[...], w_theirs[at : at + width, lanes], ((1,), (0,)))
                total = term if total is None else total + term
                at += width
            stage[t] = (gate_ref[gate_row, lanes] * total).astype(jnp.bfloat16)
            copy(t).start()

    @pl.when(straight)
    def _():
        run(w_own, w_back)

    @pl.when(jnp.logical_not(straight))
    def _():
        run(w_mate, w_far)

    for t in range(tiles):
        copy(t).wait()


def project(step_index, mine, theirs, weights, gate_table):
    rows, columns = mine[0].shape[0], weights[0].shape[1]
    tile = 512
    operands = [*mine, *theirs, *weights, gate_table]
    return pl.pallas_call(
        functools.partial(project_kernel, len(mine), tile),
        out_shape=jax.ShapeDtypeStruct((rows, columns), jnp.bfloat16),
        in_specs=[pl.BlockSpec(memory_space=pltpu.SMEM)]
        + [pl.BlockSpec(memory_space=pltpu.VMEM)] * len(operands),
        out_specs=pl.BlockSpec(memory_space=pl.ANY),
        scratch_shapes=[
            pltpu.VMEM((columns // tile, rows, tile), jnp.bfloat16),
            pltpu.SemaphoreType.DMA((columns // tile,)),
        ],
        compiler_params=pltpu.CompilerParams(vmem_limit_bytes=VMEM_LIMIT),
        cost_estimate=BRIEF,
        name="project",
    )(step_index, *operands)


def after(value, done):
    return lax.optimization_barrier((value, done))[0]


def swap_pairs(count):
    return [(i, count - 1 - i) for i in range(count)]


def on_device(query_rows, key_rows, value_rows, out_weight, gate_table, step_index, block_mask):
    heads = query_rows.shape[1] // HD
    spans, cores, sides = lax.axis_size("span"), lax.axis_size("seq"), lax.axis_size("head")
    split = (heads + 1) // 2
    groups = [(0, split), (split, heads)]
    everyone = (0, heads)
    exchange = sides == cores == 2
    final = spans - 2

    def up(x, step):
        return lax.ppermute(x, "span", [(i, i + 1) for i in range(step - 1, spans - 2)])

    def across(x):
        return lax.ppermute(x, "seq", swap_pairs(cores))

    if exchange:
        pair = ("head", "seq")
        w_far = lax.ppermute(out_weight, pair, [(1, 2), (2, 1)])
    asked = lax.ppermute(query_rows, "span", [(spans - 1, spans - 2)])
    queries = [query_rows, across(query_rows)]
    key, value = key_rows, value_rows
    own = lent = None
    for step in range(final):
        key_next = up(key, step + 1)
        if step + 1 < final:
            value_next = up(value, step + 1)
        else:
            value_next = [up(value[:, a * HD : b * HD], step + 1) for a, b in groups]
        if step == 0:
            (own,) = attend(block_mask, ["own"], 0, everyone, key, [value], queries, [])
            asked = after(asked, own)
            asks = [asked, across(asked)]
            (lent,) = attend(block_mask, ["lent"], 0, everyone, key, [value], asks, [])
            key_next = after(key_next, own)
        else:
            lent, own = attend(
                block_mask, ["lent", "own"], step, everyone, key, [value], asks + queries, [lent, own]
            )
        key = key_next
        value = after(value_next, lent) if step + 1 < final else [after(x, lent) for x in value_next]
    sent, back_up, drafts = [], [(spans - 2, spans - 1)], []
    for g, part in enumerate(groups):
        piece = after(value[g], message) if g else value[g]
        (lent,), draft = attend(block_mask, ["lent"], final, part, key, [piece], asks, [lent], emit=True)
        message = join(block_mask, part, lent, across(draft))
        sent.append(lax.ppermute(message, "span", back_up))
    queries[0] = after(queries[0], message)
    (own,), draft = attend(block_mask, ["own"], final, everyone, key, value, queries, [own], emit=True)
    mate = across(draft)
    mine = [join(block_mask, groups[0], own, mate, sent[0])]
    mine.append(join(block_mask, groups[1], own, mate, after(sent[1], mine[0])))

    if exchange:
        theirs = [lax.ppermute(x, "head", swap_pairs(sides)) for x in mine]
        w_mate = lax.ppermute(after(out_weight, message), pair, [(0, 1), (3, 2)])
        w_back = lax.ppermute(after(w_far, own), pair, [(1, 0), (2, 3)])
        return project(step_index, mine, theirs, [out_weight, w_mate, w_far, w_back], gate_table)
    weight = lax.all_gather(out_weight, "seq", axis=1, tiled=True)
    projected = jnp.dot(jnp.concatenate(mine, axis=1), weight, preferred_element_type=jnp.float32)
    shared = lax.psum_scatter(projected.astype(jnp.bfloat16), "head", scatter_dimension=1, tiled=True)
    gate_row = gate_table[step_index[lax.axis_index("span")]]
    return (gate_row[None, :] * shared.astype(jnp.float32)).astype(jnp.bfloat16)


def solution(mesh):
    in_specs = (
        P(("streams", "span", "seq"), "head"),
        P(("streams", "span", "seq"), "head"),
        P(("streams", "span", "seq"), "head"),
        P("head", "seq"),
        P(None, "head"),
        P("streams"),
        P("streams", None),
    )
    out_specs = P(("streams", "span", "seq"), "head")
    return jax.shard_map(
        on_device, mesh=mesh, in_specs=in_specs, out_specs=out_specs, check_vma=False
    )
```

```python
import functools
import math

import jax
import jax.numpy as jnp
from jax import lax
from jax.experimental import pallas as pl
from jax.experimental.pallas import tpu as pltpu
from jax.sharding import PartitionSpec as P

HD = 128
NEG = -1e30
STAT = 16
VMEM_LIMIT = 16 * 1024 * 1024
BRIEF = pl.CostEstimate(flops=1, transcendentals=0, bytes_accessed=1)


def dot(a, b, dims):
    return lax.dot_general(a, b, (dims, ((), ())), preferred_element_type=jnp.float32)


def parts_of(x):
    hi = x.astype(jnp.bfloat16)
    rest = x - hi.astype(jnp.float32)
    mid = rest.astype(jnp.bfloat16)
    low = (rest - mid.astype(jnp.float32)).astype(jnp.bfloat16)
    return hi, mid, low


def write_message(acc, top, out_ref, at):
    rows = acc.shape[0]
    lanes = slice(at, at + HD)
    total = acc[:, HD:]
    live = total > 0.0
    safe = jnp.where(live, total, 1.0)
    out_ref[0:rows, lanes] = (acc[:, :HD] / safe).astype(jnp.bfloat16)
    lse = jnp.where(live, top + jnp.log2(safe), NEG)
    hi, mid, low = parts_of(lse)
    lane = lax.broadcasted_iota(jnp.int32, lse.shape, 1)
    zero = jnp.zeros_like(hi)
    packed = jnp.where(lane == 0, hi, jnp.where(lane == 1, mid, jnp.where(lane == 2, low, zero)))
    row = lax.broadcasted_iota(jnp.int32, (STAT, HD), 0)
    col = lax.broadcasted_iota(jnp.int32, (STAT, HD), 1)
    stats = jnp.zeros((STAT, HD), jnp.float32)
    for block in range(rows // HD):
        pick = jnp.where((row - 3 * block == col) & (col < 3), 1.0, 0.0).astype(jnp.bfloat16)
        stats += dot(pick, packed[block * HD : (block + 1) * HD], ((1,), (1,)))
    out_ref[rows:, lanes] = stats.astype(jnp.bfloat16)


def read_message(msg_ref, rows, at):
    lanes = slice(at, at + HD)
    row = lax.broadcasted_iota(jnp.int32, (STAT, HD), 0)
    blocks = []
    for block in range(rows // HD):
        pick = jnp.where((row >= 3 * block) & (row < 3 * block + 3), 1.0, 0.0).astype(jnp.bfloat16)
        blocks.append(dot(msg_ref[rows:, lanes], pick, ((0,), (0,))))
    return msg_ref[0:rows, lanes].astype(jnp.float32), jnp.concatenate(blocks, axis=0)


def visible_of(role, step, mask_ref):
    span, spans = lax.axis_index("span"), mask_ref.shape[1]
    keys = jnp.maximum(span - step, 0)
    if role == "own":
        there = (span >= step) if step == 0 else (span >= step) & (span != spans - 1)
        return there & (mask_ref[span, keys] == 1)
    return (span == spans - 2) & (span >= step) & (mask_ref[spans - 1, keys] == 1)


def wide(h):
    return slice(2 * h * HD, 2 * (h + 1) * HD)


def update(q, keys, values, acc, top):
    scale = math.log2(math.e) / math.sqrt(HD)
    scores = [dot(q, k, ((1,), (1,))) for k in keys]
    peak = functools.reduce(jnp.maximum, scores) if len(scores) > 1 else scores[0]
    peak = jnp.broadcast_to(jnp.max(peak, axis=1, keepdims=True) * scale, (q.shape[0], HD))
    new_top = peak if top is None else jnp.maximum(top, peak)
    total = None
    for score, v in zip(scores, values):
        line = jnp.concatenate([new_top] * (v.shape[0] // HD), axis=1)
        prob = jnp.exp2(score * scale - line).astype(jnp.bfloat16)
        wide_v = jnp.concatenate([v, jnp.ones(v.shape, jnp.bfloat16)], axis=1)
        term = dot(prob, wide_v, ((1,), (0,)))
        total = term if total is None else total + term
    if top is not None:
        fade = jnp.exp2(top - new_top)
        total += acc * jnp.concatenate([fade, fade], axis=1)
    return total, new_top


def merge(acc, top, part, lse):
    peak = jnp.maximum(top, lse)
    mine = jnp.exp2(top - peak)
    theirs = jnp.where(lse > 0.5 * NEG, jnp.exp2(lse - peak), 0.0)
    return (
        acc * jnp.concatenate([mine, mine], axis=1) + jnp.concatenate([part * theirs, theirs], axis=1),
        peak,
    )


def tall(h):
    return slice(h * HD, (h + 1) * HD)


def attend_kernel(roles, step, emit, mask_ref, k_ref, v_ref, *refs):
    q_refs, refs = refs[: 2 * len(roles)], refs[2 * len(roles) :]
    if step:
        refs = refs[2 * len(roles) :]
    drafts = refs[2 * len(roles) :]
    rows, heads = q_refs[0].shape[0], k_ref.shape[1] // HD
    for i, role in enumerate(roles):
        acc_ref, top_ref = refs[2 * i : 2 * i + 2]
        visible = visible_of(role, step, mask_ref)

        @pl.when(visible)
        def _():
            for h in range(heads):
                for half in range(2):
                    at = slice(half * rows, (half + 1) * rows)
                    acc, top = (acc_ref[at, wide(h)], top_ref[at, tall(h)]) if step else (None, None)
                    acc, top = update(q_refs[2 * i + half][:, tall(h)], [k_ref[:, tall(h)]], [v_ref[:, tall(h)]], acc, top)
                    acc_ref[at, wide(h)] = acc
                    top_ref[at, tall(h)] = top

        if step == 0:

            @pl.when(jnp.logical_not(visible))
            def _():
                acc_ref[...] = jnp.zeros(acc_ref.shape, jnp.float32)
                top_ref[...] = jnp.full(top_ref.shape, NEG, jnp.float32)

        if emit:
            def write():
                for h in range(heads):
                    write_message(acc_ref[rows:, wide(h)], top_ref[rows:, tall(h)], drafts[i], h * HD)

            if role == "lent":
                pl.when(lax.axis_index("span") == mask_ref.shape[1] - 2)(write)
            else:
                write()


def call(kernel, name, out_shape, mask, operands, aliases=None):
    return pl.pallas_call(
        kernel,
        out_shape=out_shape,
        in_specs=[pl.BlockSpec(memory_space=pltpu.SMEM)] + [pl.BlockSpec(memory_space=pltpu.VMEM)] * len(operands),
        out_specs=[pl.BlockSpec(memory_space=pltpu.VMEM)] * len(out_shape),
        input_output_aliases=aliases or {},
        compiler_params=pltpu.CompilerParams(vmem_limit_bytes=VMEM_LIMIT),
        cost_estimate=BRIEF,
        name=name,
    )(mask, *operands)


def state_shape(rows, width):
    return [
        jax.ShapeDtypeStruct((rows, 2 * width), jnp.float32),
        jax.ShapeDtypeStruct((rows, width), jnp.float32),
    ]


def message_shape(rows, heads):
    return jax.ShapeDtypeStruct((rows + STAT, heads * HD), jnp.bfloat16)


def attend(mask, roles, step, key, value, queries, states, emit):
    rows, width = key.shape
    out_shape = state_shape(2 * rows, width) * len(roles)
    if emit:
        out_shape = out_shape + [message_shape(rows, width // HD)] * len(roles)
    operands = [key, value, *queries]
    aliases = {}
    if step:
        aliases = {1 + len(operands) + i: i for i in range(2 * len(roles))}
        for state in states:
            operands += list(state)
    kernel = functools.partial(attend_kernel, roles, step, emit)
    out = call(kernel, "attend_" + "_".join(roles) + str(step), out_shape, mask, operands, aliases)
    return [tuple(out[2 * i : 2 * i + 2]) for i in range(len(roles))], out[2 * len(roles) :]


def fold_kernel(roles, mask_ref, *refs):
    count = len(roles)
    for i, role in enumerate(roles):
        acc_in, top_in, mate_ref = refs[3 * i : 3 * i + 3]
        acc_ref, top_ref = refs[3 * count + 2 * i : 3 * count + 2 * i + 2]
        rows = acc_ref.shape[0]

        def run():
            for h in range(top_ref.shape[1] // HD):
                part, lse = read_message(mate_ref, rows, h * HD)
                acc, top = merge(acc_in[0:rows, wide(h)], top_in[0:rows, tall(h)], part, lse)
                acc_ref[:, wide(h)] = acc
                top_ref[:, tall(h)] = top

        if role == "lent":
            pl.when(lax.axis_index("span") == mask_ref.shape[1] - 2)(run)
        else:
            run()


def fold(mask, roles, states, mates):
    rows, width = mates[0].shape[0] - STAT, mates[0].shape[1]
    operands = [x for state, mate in zip(states, mates) for x in (*state, mate)]
    kernel = functools.partial(fold_kernel, roles)
    out = call(kernel, "fold", state_shape(rows, width) * len(roles), mask, operands)
    return [tuple(out[2 * i : 2 * i + 2]) for i in range(len(roles))]


def last_kernel(role, step, groups, mask_ref, ka_ref, kb_ref, va_ref, vb_ref, q_ref, acc_in, top_in, *outs):
    rows = q_ref.shape[0]
    visible = visible_of(role, step, mask_ref)

    def store(h, acc, top):
        if role == "own":
            outs[0][:, wide(h)] = acc
            outs[1][:, tall(h)] = top
        else:
            g = 0 if h < groups[1][0] else 1
            write_message(acc, top, outs[g], (h - groups[g][0]) * HD)

    def run(see):
        for h in range(q_ref.shape[1] // HD):
            acc, top = acc_in[:, wide(h)], top_in[:, tall(h)]
            if see:
                keys, values = [ka_ref[:, tall(h)], kb_ref[:, tall(h)]], [va_ref[:, tall(h)], vb_ref[:, tall(h)]]
                acc, top = update(q_ref[:, tall(h)], keys, values, acc, top)
            store(h, acc, top)

    helps = lax.axis_index("span") == mask_ref.shape[1] - 2
    pl.when(visible)(lambda: run(True))
    pl.when(jnp.logical_not(visible) & (helps if role == "lent" else True))(lambda: run(False))


def attend_last(mask, role, step, groups, keys, values, query, state):
    rows, width = query.shape
    if role == "own":
        out_shape = state_shape(rows, width)
    else:
        out_shape = [message_shape(rows, b - a) for a, b in groups]
    kernel = functools.partial(last_kernel, role, step, groups)
    return call(kernel, "last_" + role, out_shape, mask, [*keys, *values, query, *state])


def join_kernel(part_of_heads, mask_ref, acc_ref, top_ref, msg_ref, out_ref):
    low, high = part_of_heads
    rows = acc_ref.shape[0]

    def run(helped):
        for h in range(low, high):
            acc = acc_ref[:, wide(h)]
            if helped:
                part, lse = read_message(msg_ref, rows, (h - low) * HD)
                acc, _ = merge(acc, top_ref[:, tall(h)], part, lse)
            out_ref[:, tall(h - low)] = (acc[:, :HD] / acc[:, HD:]).astype(jnp.bfloat16)

    helped = lax.axis_index("span") == mask_ref.shape[1] - 1
    pl.when(helped)(lambda: run(True))
    pl.when(jnp.logical_not(helped))(lambda: run(False))


def join(mask, part_of_heads, state, message):
    shape = (state[0].shape[0], (part_of_heads[1] - part_of_heads[0]) * HD)
    kernel = functools.partial(join_kernel, part_of_heads)
    return call(kernel, "join" + str(part_of_heads[0]), [jax.ShapeDtypeStruct(shape, jnp.bfloat16)], mask, [*state, message])[0]


def project_kernel(groups, tile, step_ref, *refs):
    mine, theirs = refs[:groups], refs[groups : 2 * groups]
    w_own, w_mate, w_far, w_back, gate_ref, out_ref, stage, sems = refs[2 * groups :]
    straight = lax.axis_index("head") == lax.axis_index("seq")
    tiles = out_ref.shape[1] // tile
    gate_row = pl.ds(step_ref[lax.axis_index("span")], 1)

    def copy(t):
        return pltpu.make_async_copy(stage.at[t], out_ref.at[:, t * tile : (t + 1) * tile], sems.at[t])

    def run(w_mine, w_theirs):
        for t in range(tiles):
            lanes = slice(t * tile, (t + 1) * tile)
            total, at = None, 0
            for own_ref, far_ref in zip(mine, theirs):
                width = own_ref.shape[1]
                term = dot(own_ref[...], w_mine[at : at + width, lanes], ((1,), (0,)))
                term += dot(far_ref[...], w_theirs[at : at + width, lanes], ((1,), (0,)))
                total = term if total is None else total + term
                at += width
            stage[t] = (gate_ref[gate_row, lanes] * total).astype(jnp.bfloat16)
            copy(t).start()

    @pl.when(straight)
    def _():
        run(w_own, w_back)

    @pl.when(jnp.logical_not(straight))
    def _():
        run(w_mate, w_far)

    for t in range(tiles):
        copy(t).wait()


def project(step_index, mine, theirs, weights, gate_table):
    rows, columns = mine[0].shape[0], weights[0].shape[1]
    tile = 512
    operands = [*mine, *theirs, *weights, gate_table]
    return pl.pallas_call(
        functools.partial(project_kernel, len(mine), tile),
        out_shape=jax.ShapeDtypeStruct((rows, columns), jnp.bfloat16),
        in_specs=[pl.BlockSpec(memory_space=pltpu.SMEM)]
        + [pl.BlockSpec(memory_space=pltpu.VMEM)] * len(operands),
        out_specs=pl.BlockSpec(memory_space=pl.ANY),
        scratch_shapes=[
            pltpu.VMEM((columns // tile, rows, tile), jnp.bfloat16),
            pltpu.SemaphoreType.DMA((columns // tile,)),
        ],
        compiler_params=pltpu.CompilerParams(vmem_limit_bytes=VMEM_LIMIT),
        cost_estimate=BRIEF,
        name="project",
    )(step_index, *operands)


def after(value, done):
    return lax.optimization_barrier((value, done))[0]


def swap_pairs(count):
    return [(i, count - 1 - i) for i in range(count)]


def on_device(query_rows, key_rows, value_rows, out_weight, gate_table, step_index, block_mask):
    heads = query_rows.shape[1] // HD
    spans, cores, sides = lax.axis_size("span"), lax.axis_size("seq"), lax.axis_size("head")
    split = (heads + 1) // 2
    groups = [(0, split), (split, heads)]
    exchange = sides == cores == 2
    final = spans - 2

    def up(x, step):
        return lax.ppermute(x, "span", [(i, i + 1) for i in range(step - 1, spans - 2)])

    def across(x):
        return lax.ppermute(x, "seq", swap_pairs(cores))

    if exchange:
        pair = ("head", "seq")
        w_far = lax.ppermute(out_weight, pair, [(1, 2), (2, 1)])
    asked = lax.ppermute(query_rows, "span", [(spans - 1, spans - 2)])
    query_mate = across(query_rows)
    if exchange:
        w_mate = lax.ppermute(out_weight, pair, [(0, 1), (3, 2)])
        query_mate = after(query_mate, w_mate)
    queries, lent = [query_rows, query_mate], None
    key, value = key_rows, value_rows
    roles = ["lent", "own"]
    for step in range(final):
        key_next, value_next = up(key, step + 1), up(value, step + 1)
        emit = step + 1 == final
        if step == 0:
            (own,), own_draft = attend(block_mask, ["own"], 0, key, value, queries, [], emit)
            asked = after(asked, own)
            asks = [asked, across(asked)]
            (lent,), lent_draft = attend(block_mask, ["lent"], 0, key, value, asks, [], emit)
            states, drafts = [lent, own], [*lent_draft, *own_draft]
        else:
            states, drafts = attend(block_mask, roles, step, key, value, asks + queries, states, emit)
        key, value = key_next, value_next
    lent, own = fold(block_mask, roles, states, [across(x) for x in drafts])
    keys = [key, across(key)]
    values = [value, across(value)]
    back_up = [(spans - 2, spans - 1)]
    messages = attend_last(block_mask, "lent", final, groups, keys, values, asks[0], lent)
    sent = [lax.ppermute(x, "span", back_up) for x in messages]
    if exchange:
        w_back = lax.ppermute(after(w_far, messages[1]), pair, [(1, 0), (2, 3)])
    own = attend_last(block_mask, "own", final, groups, keys, values, after(query_rows, messages), own)
    mine = [join(block_mask, groups[0], own, sent[0])]
    mine.append(join(block_mask, groups[1], own, after(sent[1], mine[0])))

    if exchange:
        theirs = [lax.ppermute(x, "head", swap_pairs(sides)) for x in mine]
        return project(step_index, mine, theirs, [out_weight, w_mate, w_far, w_back], gate_table)
    weight = lax.all_gather(out_weight, "seq", axis=1, tiled=True)
    projected = jnp.dot(jnp.concatenate(mine, axis=1), weight, preferred_element_type=jnp.float32)
    shared = lax.psum_scatter(projected.astype(jnp.bfloat16), "head", scatter_dimension=1, tiled=True)
    gate_row = gate_table[step_index[lax.axis_index("span")]]
    return (gate_row[None, :] * shared.astype(jnp.float32)).astype(jnp.bfloat16)


def solution(mesh):
    in_specs = (
        P(("streams", "span", "seq"), "head"),
        P(("streams", "span", "seq"), "head"),
        P(("streams", "span", "seq"), "head"),
        P("head", "seq"),
        P(None, "head"),
        P("streams"),
        P("streams", None),
    )
    out_specs = P(("streams", "span", "seq"), "head")
    return jax.shard_map(
        on_device, mesh=mesh, in_specs=in_specs, out_specs=out_specs, check_vma=False
    )
```

```python
import functools
import math

import jax
import jax.numpy as jnp
from jax import lax
from jax.experimental import pallas as pl
from jax.experimental.pallas import tpu as pltpu
from jax.sharding import PartitionSpec as P

HD = 128
NEG = -1e30
STAT = 16
VMEM_LIMIT = 16 * 1024 * 1024
BRIEF = pl.CostEstimate(flops=1, transcendentals=0, bytes_accessed=1)


def dot(a, b, dims):
    return lax.dot_general(a, b, (dims, ((), ())), preferred_element_type=jnp.float32)


def parts_of(x):
    hi = x.astype(jnp.bfloat16)
    rest = x - hi.astype(jnp.float32)
    mid = rest.astype(jnp.bfloat16)
    low = (rest - mid.astype(jnp.float32)).astype(jnp.bfloat16)
    return hi, mid, low


def write_message(acc, top, out_ref, at):
    rows = acc.shape[0]
    lanes = slice(at, at + HD)
    total = acc[:, HD:]
    live = total > 0.0
    safe = jnp.where(live, total, 1.0)
    out_ref[0:rows, lanes] = (acc[:, :HD] / safe).astype(jnp.bfloat16)
    lse = jnp.where(live, top + jnp.log2(safe), NEG)
    hi, mid, low = parts_of(lse)
    lane = lax.broadcasted_iota(jnp.int32, lse.shape, 1)
    zero = jnp.zeros_like(hi)
    packed = jnp.where(lane == 0, hi, jnp.where(lane == 1, mid, jnp.where(lane == 2, low, zero)))
    row = lax.broadcasted_iota(jnp.int32, (STAT, HD), 0)
    col = lax.broadcasted_iota(jnp.int32, (STAT, HD), 1)
    stats = jnp.zeros((STAT, HD), jnp.float32)
    for block in range(rows // HD):
        pick = jnp.where((row - 3 * block == col) & (col < 3), 1.0, 0.0).astype(jnp.bfloat16)
        stats += dot(pick, packed[block * HD : (block + 1) * HD], ((1,), (1,)))
    out_ref[rows:, lanes] = stats.astype(jnp.bfloat16)


def read_message(msg_ref, rows, at):
    lanes = slice(at, at + HD)
    row = lax.broadcasted_iota(jnp.int32, (STAT, HD), 0)
    blocks = []
    for block in range(rows // HD):
        pick = jnp.where((row >= 3 * block) & (row < 3 * block + 3), 1.0, 0.0).astype(jnp.bfloat16)
        blocks.append(dot(msg_ref[rows:, lanes], pick, ((0,), (0,))))
    return msg_ref[0:rows, lanes].astype(jnp.float32), jnp.concatenate(blocks, axis=0)


def visible_of(role, step, mask_ref):
    span, spans = lax.axis_index("span"), mask_ref.shape[1]
    keys = jnp.maximum(span - step, 0)
    if role == "own":
        there = (span >= step) if step == 0 else (span >= step) & (span != spans - 1)
        return there & (mask_ref[span, keys] == 1)
    return (span == spans - 2) & (span >= step) & (mask_ref[spans - 1, keys] == 1)


def wide(h):
    return slice(2 * h * HD, 2 * (h + 1) * HD)


def update(q, keys, values, acc, top):
    scale = math.log2(math.e) / math.sqrt(HD)
    scores = [dot(q, k, ((1,), (1,))) for k in keys]
    peak = functools.reduce(jnp.maximum, scores) if len(scores) > 1 else scores[0]
    peak = jnp.broadcast_to(jnp.max(peak, axis=1, keepdims=True) * scale, (q.shape[0], HD))
    new_top = peak if top is None else jnp.maximum(top, peak)
    total = None
    for score, v in zip(scores, values):
        line = jnp.concatenate([new_top] * (v.shape[0] // HD), axis=1)
        prob = jnp.exp2(score * scale - line).astype(jnp.bfloat16)
        wide_v = jnp.concatenate([v, jnp.ones(v.shape, jnp.bfloat16)], axis=1)
        term = dot(prob, wide_v, ((1,), (0,)))
        total = term if total is None else total + term
    if top is not None:
        fade = jnp.exp2(top - new_top)
        total += acc * jnp.concatenate([fade, fade], axis=1)
    return total, new_top


def merge(acc, top, part, lse):
    peak = jnp.maximum(top, lse)
    mine = jnp.exp2(top - peak)
    theirs = jnp.where(lse > 0.5 * NEG, jnp.exp2(lse - peak), 0.0)
    return (
        acc * jnp.concatenate([mine, mine], axis=1) + jnp.concatenate([part * theirs, theirs], axis=1),
        peak,
    )


def tall(h):
    return slice(h * HD, (h + 1) * HD)


def attend_kernel(roles, step, emit, mask_ref, k_ref, v_ref, *refs):
    q_refs, refs = refs[: 2 * len(roles)], refs[2 * len(roles) :]
    if step:
        refs = refs[2 * len(roles) :]
    drafts = refs[2 * len(roles) :]
    rows, heads = q_refs[0].shape[0], k_ref.shape[1] // HD
    for i, role in enumerate(roles):
        acc_ref, top_ref = refs[2 * i : 2 * i + 2]
        visible = visible_of(role, step, mask_ref)

        @pl.when(visible)
        def _():
            for h in range(heads):
                for half in range(2):
                    at = slice(half * rows, (half + 1) * rows)
                    acc, top = (acc_ref[at, wide(h)], top_ref[at, tall(h)]) if step else (None, None)
                    acc, top = update(q_refs[2 * i + half][:, tall(h)], [k_ref[:, tall(h)]], [v_ref[:, tall(h)]], acc, top)
                    acc_ref[at, wide(h)] = acc
                    top_ref[at, tall(h)] = top

        if step == 0:

            @pl.when(jnp.logical_not(visible))
            def _():
                acc_ref[...] = jnp.zeros(acc_ref.shape, jnp.float32)
                top_ref[...] = jnp.full(top_ref.shape, NEG, jnp.float32)

        if emit:
            def write():
                for h in range(heads):
                    write_message(acc_ref[rows:, wide(h)], top_ref[rows:, tall(h)], drafts[i], h * HD)

            if role == "lent":
                pl.when(lax.axis_index("span") == mask_ref.shape[1] - 2)(write)
            else:
                write()


def call(kernel, name, out_shape, mask, operands, aliases=None):
    return pl.pallas_call(
        kernel,
        out_shape=out_shape,
        in_specs=[pl.BlockSpec(memory_space=pltpu.SMEM)] + [pl.BlockSpec(memory_space=pltpu.VMEM)] * len(operands),
        out_specs=[pl.BlockSpec(memory_space=pltpu.VMEM)] * len(out_shape),
        input_output_aliases=aliases or {},
        compiler_params=pltpu.CompilerParams(vmem_limit_bytes=VMEM_LIMIT),
        cost_estimate=BRIEF,
        name=name,
    )(mask, *operands)


def state_shape(rows, width):
    return [
        jax.ShapeDtypeStruct((rows, 2 * width), jnp.float32),
        jax.ShapeDtypeStruct((rows, width), jnp.float32),
    ]


def message_shape(rows, heads):
    return jax.ShapeDtypeStruct((rows + STAT, heads * HD), jnp.bfloat16)


def attend(mask, roles, step, key, value, queries, states, emit):
    rows, width = key.shape
    out_shape = state_shape(2 * rows, width) * len(roles)
    if emit:
        out_shape = out_shape + [message_shape(rows, width // HD)] * len(roles)
    operands = [key, value, *queries]
    aliases = {}
    if step:
        aliases = {1 + len(operands) + i: i for i in range(2 * len(roles))}
        for state in states:
            operands += list(state)
    kernel = functools.partial(attend_kernel, roles, step, emit)
    out = call(kernel, "attend_" + "_".join(roles) + str(step), out_shape, mask, operands, aliases)
    return [tuple(out[2 * i : 2 * i + 2]) for i in range(len(roles))], out[2 * len(roles) :]


def fold_kernel(roles, mask_ref, *refs):
    count = len(roles)
    for i, role in enumerate(roles):
        acc_in, top_in, mate_ref = refs[3 * i : 3 * i + 3]
        acc_ref, top_ref = refs[3 * count + 2 * i : 3 * count + 2 * i + 2]
        rows = acc_ref.shape[0]

        def run():
            for h in range(top_ref.shape[1] // HD):
                part, lse = read_message(mate_ref, rows, h * HD)
                acc, top = merge(acc_in[0:rows, wide(h)], top_in[0:rows, tall(h)], part, lse)
                acc_ref[:, wide(h)] = acc
                top_ref[:, tall(h)] = top

        if role == "lent":
            pl.when(lax.axis_index("span") == mask_ref.shape[1] - 2)(run)
        else:
            run()


def fold(mask, roles, states, mates):
    rows, width = mates[0].shape[0] - STAT, mates[0].shape[1]
    operands = [x for state, mate in zip(states, mates) for x in (*state, mate)]
    kernel = functools.partial(fold_kernel, roles)
    out = call(kernel, "fold", state_shape(rows, width) * len(roles), mask, operands)
    return [tuple(out[2 * i : 2 * i + 2]) for i in range(len(roles))]


def last_kernel(role, step, groups, mask_ref, ka_ref, kb_ref, va_ref, vb_ref, q_ref, acc_in, top_in, *outs):
    rows = q_ref.shape[0]
    visible = visible_of(role, step, mask_ref)

    def store(h, acc, top):
        if role == "own":
            outs[0][:, wide(h)] = acc
            outs[1][:, tall(h)] = top
        else:
            g = 0 if h < groups[1][0] else 1
            write_message(acc, top, outs[g], (h - groups[g][0]) * HD)

    def run(see):
        for h in range(q_ref.shape[1] // HD):
            acc, top = acc_in[:, wide(h)], top_in[:, tall(h)]
            if see:
                keys, values = [ka_ref[:, tall(h)], kb_ref[:, tall(h)]], [va_ref[:, tall(h)], vb_ref[:, tall(h)]]
                acc, top = update(q_ref[:, tall(h)], keys, values, acc, top)
            store(h, acc, top)

    helps = lax.axis_index("span") == mask_ref.shape[1] - 2
    pl.when(visible)(lambda: run(True))
    pl.when(jnp.logical_not(visible) & (helps if role == "lent" else True))(lambda: run(False))


def attend_last(mask, role, step, groups, keys, values, query, state):
    rows, width = query.shape
    if role == "own":
        out_shape = state_shape(rows, width)
    else:
        out_shape = [message_shape(rows, b - a) for a, b in groups]
    kernel = functools.partial(last_kernel, role, step, groups)
    return call(kernel, "last_" + role, out_shape, mask, [*keys, *values, query, *state])


def join_kernel(part_of_heads, mask_ref, acc_ref, top_ref, msg_ref, out_ref):
    low, high = part_of_heads
    rows = acc_ref.shape[0]

    def run(helped):
        for h in range(low, high):
            acc = acc_ref[:, wide(h)]
            if helped:
                part, lse = read_message(msg_ref, rows, (h - low) * HD)
                acc, _ = merge(acc, top_ref[:, tall(h)], part, lse)
            out_ref[:, tall(h - low)] = (acc[:, :HD] / acc[:, HD:]).astype(jnp.bfloat16)

    helped = lax.axis_index("span") == mask_ref.shape[1] - 1
    pl.when(helped)(lambda: run(True))
    pl.when(jnp.logical_not(helped))(lambda: run(False))


def join(mask, part_of_heads, state, message):
    shape = (state[0].shape[0], (part_of_heads[1] - part_of_heads[0]) * HD)
    kernel = functools.partial(join_kernel, part_of_heads)
    return call(kernel, "join" + str(part_of_heads[0]), [jax.ShapeDtypeStruct(shape, jnp.bfloat16)], mask, [*state, message])[0]


TILE = 512


def project_kernel(lows, step_ref, *refs):
    count = len(lows)
    rows_refs, (w_own, w_mate, w_far, w_back), refs = refs[:count], refs[count : count + 4], refs[count + 4 :]
    straight = lax.axis_index("head") == lax.axis_index("seq")
    last = len(refs) > 1
    if last:
        total_ref, gate_ref, out_ref, stage, sems = refs
        gate_row = pl.ds(step_ref[lax.axis_index("span")], 1)
    else:
        out_ref = refs[0]
    tiles = out_ref.shape[1] // TILE

    def copy(t):
        return pltpu.make_async_copy(stage.at[t], out_ref.at[:, t * TILE : (t + 1) * TILE], sems.at[t])

    def run(w_mine, w_theirs):
        for t in range(tiles):
            lanes = slice(t * TILE, (t + 1) * TILE)
            total = total_ref[:, lanes] if last else None
            for ref, (low, own) in zip(rows_refs, lows):
                weight = w_mine if own else w_theirs
                term = dot(ref[...], weight[low : low + ref.shape[1], lanes], ((1,), (0,)))
                total = term if total is None else total + term
            if last:
                stage[t] = (gate_ref[gate_row, lanes] * total).astype(jnp.bfloat16)
                copy(t).start()
            else:
                out_ref[:, lanes] = total

    pl.when(straight)(lambda: run(w_own, w_back))
    pl.when(jnp.logical_not(straight))(lambda: run(w_mate, w_far))
    if last:
        for t in range(tiles):
            copy(t).wait()


def project(step_index, terms, weights, total=None, gate_table=None):
    rows, columns = terms[0][0].shape[0], weights[0].shape[1]
    last = total is not None
    operands = [x for x, _, _ in terms] + [*weights] + ([total, gate_table] if last else [])
    return pl.pallas_call(
        functools.partial(project_kernel, [(low, own) for _, low, own in terms]),
        out_shape=jax.ShapeDtypeStruct((rows, columns), jnp.bfloat16 if last else jnp.float32),
        in_specs=[pl.BlockSpec(memory_space=pltpu.SMEM)]
        + [pl.BlockSpec(memory_space=pltpu.VMEM)] * len(operands),
        out_specs=pl.BlockSpec(memory_space=pl.ANY if last else pltpu.VMEM),
        scratch_shapes=[
            pltpu.VMEM((columns // TILE, rows, TILE), jnp.bfloat16),
            pltpu.SemaphoreType.DMA((columns // TILE,)),
        ]
        if last
        else [],
        compiler_params=pltpu.CompilerParams(vmem_limit_bytes=VMEM_LIMIT),
        cost_estimate=BRIEF,
        name="project_last" if last else "project_most",
    )(step_index, *operands)


def after(value, done):
    return lax.optimization_barrier((value, done))[0]


def swap_pairs(count):
    return [(i, count - 1 - i) for i in range(count)]


def on_device(query_rows, key_rows, value_rows, out_weight, gate_table, step_index, block_mask):
    heads = query_rows.shape[1] // HD
    spans, cores, sides = lax.axis_size("span"), lax.axis_size("seq"), lax.axis_size("head")
    split = (heads + 1) // 2
    groups = [(0, split), (split, heads)]
    exchange = sides == cores == 2
    final = spans - 2

    def up(x, step):
        return lax.ppermute(x, "span", [(i, i + 1) for i in range(step - 1, spans - 2)])

    def across(x):
        return lax.ppermute(x, "seq", swap_pairs(cores))

    if exchange:
        pair = ("head", "seq")
        w_far = lax.ppermute(out_weight, pair, [(1, 2), (2, 1)])
    asked = lax.ppermute(query_rows, "span", [(spans - 1, spans - 2)])
    query_mate = across(query_rows)
    if exchange:
        w_mate = across(out_weight)
        query_mate = after(query_mate, w_mate)
    queries, lent = [query_rows, query_mate], None
    key, value = key_rows, value_rows
    roles = ["lent", "own"]
    for step in range(final):
        key_next, value_next = up(key, step + 1), up(value, step + 1)
        emit = step + 1 == final
        if step == 0:
            (own,), own_draft = attend(block_mask, ["own"], 0, key, value, queries, [], emit)
            asked = after(asked, own)
            asks = [asked, across(asked)]
            (lent,), lent_draft = attend(block_mask, ["lent"], 0, key, value, asks, [], emit)
            states, drafts = [lent, own], [*lent_draft, *own_draft]
        else:
            states, drafts = attend(block_mask, roles, step, key, value, asks + queries, states, emit)
        key, value = key_next, value_next
    lent, own = fold(block_mask, roles, states, [across(x) for x in drafts])
    keys = [key, across(key)]
    values = [value, across(value)]
    back_up = [(spans - 2, spans - 1)]
    messages = attend_last(block_mask, "lent", final, groups, keys, values, asks[0], lent)
    sent = [lax.ppermute(x, "span", back_up) for x in messages]
    if exchange:
        w_back = across(after(w_far, messages[1]))
    own = attend_last(block_mask, "own", final, groups, keys, values, after(query_rows, messages), own)
    mine = [join(block_mask, groups[0], own, sent[0])]
    mine.append(join(block_mask, groups[1], own, after(sent[1], mine[0])))

    if exchange:
        theirs = [lax.ppermute(x, "head", swap_pairs(sides)) for x in mine]
        weights, low = [out_weight, w_mate, w_far, w_back], split * HD
        most = [(mine[0], 0, True), (mine[1], low, True), (theirs[0], 0, False)]
        total = project(step_index, most, weights)
        return project(step_index, [(theirs[1], low, False)], weights, total, gate_table)
    weight = lax.all_gather(out_weight, "seq", axis=1, tiled=True)
    projected = jnp.dot(jnp.concatenate(mine, axis=1), weight, preferred_element_type=jnp.float32)
    shared = lax.psum_scatter(projected.astype(jnp.bfloat16), "head", scatter_dimension=1, tiled=True)
    gate_row = gate_table[step_index[lax.axis_index("span")]]
    return (gate_row[None, :] * shared.astype(jnp.float32)).astype(jnp.bfloat16)


def solution(mesh):
    in_specs = (
        P(("streams", "span", "seq"), "head"),
        P(("streams", "span", "seq"), "head"),
        P(("streams", "span", "seq"), "head"),
        P("head", "seq"),
        P(None, "head"),
        P("streams"),
        P("streams", None),
    )
    out_specs = P(("streams", "span", "seq"), "head")
    return jax.shard_map(
        on_device, mesh=mesh, in_specs=in_specs, out_specs=out_specs, check_vma=False
    )
```

```python
import functools
import math

import jax
import jax.numpy as jnp
from jax import lax
from jax.experimental import pallas as pl
from jax.experimental.pallas import tpu as pltpu
from jax.sharding import PartitionSpec as P

HD = 128
NEG = -1e30
STAT = 16
VMEM_LIMIT = 16 * 1024 * 1024
BRIEF = pl.CostEstimate(flops=1, transcendentals=0, bytes_accessed=1)


def dot(a, b, dims):
    return lax.dot_general(a, b, (dims, ((), ())), preferred_element_type=jnp.float32)


def parts_of(x):
    hi = x.astype(jnp.bfloat16)
    rest = x - hi.astype(jnp.float32)
    mid = rest.astype(jnp.bfloat16)
    low = (rest - mid.astype(jnp.float32)).astype(jnp.bfloat16)
    return hi, mid, low


def write_message(acc, top, out_ref, at):
    rows = acc.shape[0]
    lanes = slice(at, at + HD)
    total = acc[:, HD:]
    live = total > 0.0
    safe = jnp.where(live, total, 1.0)
    out_ref[0:rows, lanes] = (acc[:, :HD] / safe).astype(jnp.bfloat16)
    lse = jnp.where(live, top + jnp.log2(safe), NEG)
    hi, mid, low = parts_of(lse)
    lane = lax.broadcasted_iota(jnp.int32, lse.shape, 1)
    zero = jnp.zeros_like(hi)
    packed = jnp.where(lane == 0, hi, jnp.where(lane == 1, mid, jnp.where(lane == 2, low, zero)))
    row = lax.broadcasted_iota(jnp.int32, (STAT, HD), 0)
    col = lax.broadcasted_iota(jnp.int32, (STAT, HD), 1)
    stats = jnp.zeros((STAT, HD), jnp.float32)
    for block in range(rows // HD):
        pick = jnp.where((row - 3 * block == col) & (col < 3), 1.0, 0.0).astype(jnp.bfloat16)
        stats += dot(pick, packed[block * HD : (block + 1) * HD], ((1,), (1,)))
    out_ref[rows:, lanes] = stats.astype(jnp.bfloat16)


def read_message(msg_ref, rows, at):
    lanes = slice(at, at + HD)
    row = lax.broadcasted_iota(jnp.int32, (STAT, HD), 0)
    blocks = []
    for block in range(rows // HD):
        pick = jnp.where((row >= 3 * block) & (row < 3 * block + 3), 1.0, 0.0).astype(jnp.bfloat16)
        blocks.append(dot(msg_ref[rows:, lanes], pick, ((0,), (0,))))
    return msg_ref[0:rows, lanes].astype(jnp.float32), jnp.concatenate(blocks, axis=0)


def visible_of(role, step, mask_ref):
    span, spans = lax.axis_index("span"), mask_ref.shape[1]
    keys = jnp.maximum(span - step, 0)
    if role == "own":
        there = (span >= step) if step == 0 else (span >= step) & (span != spans - 1)
        return there & (mask_ref[span, keys] == 1)
    return (span == spans - 2) & (span >= step) & (mask_ref[spans - 1, keys] == 1)


def wide(h):
    return slice(2 * h * HD, 2 * (h + 1) * HD)


def update(q, keys, values, acc, top):
    scale = math.log2(math.e) / math.sqrt(HD)
    scores = [dot(q, k, ((1,), (1,))) for k in keys]
    peak = functools.reduce(jnp.maximum, scores) if len(scores) > 1 else scores[0]
    peak = jnp.broadcast_to(jnp.max(peak, axis=1, keepdims=True) * scale, (q.shape[0], HD))
    new_top = peak if top is None else jnp.maximum(top, peak)
    total = None
    for score, v in zip(scores, values):
        line = jnp.concatenate([new_top] * (v.shape[0] // HD), axis=1)
        prob = jnp.exp2(score * scale - line).astype(jnp.bfloat16)
        wide_v = jnp.concatenate([v, jnp.ones(v.shape, jnp.bfloat16)], axis=1)
        term = dot(prob, wide_v, ((1,), (0,)))
        total = term if total is None else total + term
    if top is not None:
        fade = jnp.exp2(top - new_top)
        total += acc * jnp.concatenate([fade, fade], axis=1)
    return total, new_top


def merge(acc, top, part, lse):
    peak = jnp.maximum(top, lse)
    mine = jnp.exp2(top - peak)
    theirs = jnp.where(lse > 0.5 * NEG, jnp.exp2(lse - peak), 0.0)
    return (
        acc * jnp.concatenate([mine, mine], axis=1) + jnp.concatenate([part * theirs, theirs], axis=1),
        peak,
    )


def tall(h):
    return slice(h * HD, (h + 1) * HD)


def attend_kernel(roles, step, emit, mask_ref, k_ref, v_ref, *refs):
    q_refs, refs = refs[: 2 * len(roles)], refs[2 * len(roles) :]
    if step:
        refs = refs[2 * len(roles) :]
    drafts = refs[2 * len(roles) :]
    rows, heads = q_refs[0].shape[0], k_ref.shape[1] // HD
    for i, role in enumerate(roles):
        acc_ref, top_ref = refs[2 * i : 2 * i + 2]
        visible = visible_of(role, step, mask_ref)

        @pl.when(visible)
        def _():
            for h in range(heads):
                for half in range(2):
                    at = slice(half * rows, (half + 1) * rows)
                    acc, top = (acc_ref[at, wide(h)], top_ref[at, tall(h)]) if step else (None, None)
                    acc, top = update(q_refs[2 * i + half][:, tall(h)], [k_ref[:, tall(h)]], [v_ref[:, tall(h)]], acc, top)
                    acc_ref[at, wide(h)] = acc
                    top_ref[at, tall(h)] = top

        if step == 0:

            @pl.when(jnp.logical_not(visible))
            def _():
                acc_ref[...] = jnp.zeros(acc_ref.shape, jnp.float32)
                top_ref[...] = jnp.full(top_ref.shape, NEG, jnp.float32)

        if emit:
            def write():
                for h in range(heads):
                    write_message(acc_ref[rows:, wide(h)], top_ref[rows:, tall(h)], drafts[i], h * HD)

            if role == "lent":
                pl.when(lax.axis_index("span") == mask_ref.shape[1] - 2)(write)
            else:
                write()


def call(kernel, name, out_shape, mask, operands, aliases=None):
    return pl.pallas_call(
        kernel,
        out_shape=out_shape,
        in_specs=[pl.BlockSpec(memory_space=pltpu.SMEM)] + [pl.BlockSpec(memory_space=pltpu.VMEM)] * len(operands),
        out_specs=[pl.BlockSpec(memory_space=pltpu.VMEM)] * len(out_shape),
        input_output_aliases=aliases or {},
        compiler_params=pltpu.CompilerParams(vmem_limit_bytes=VMEM_LIMIT),
        cost_estimate=BRIEF,
        name=name,
    )(mask, *operands)


def state_shape(rows, width):
    return [
        jax.ShapeDtypeStruct((rows, 2 * width), jnp.float32),
        jax.ShapeDtypeStruct((rows, width), jnp.float32),
    ]


def message_shape(rows, heads):
    return jax.ShapeDtypeStruct((rows + STAT, heads * HD), jnp.bfloat16)


def attend(mask, roles, step, key, value, queries, states, emit):
    rows, width = key.shape
    out_shape = state_shape(2 * rows, width) * len(roles)
    if emit:
        out_shape = out_shape + [message_shape(rows, width // HD)] * len(roles)
    operands = [key, value, *queries]
    aliases = {}
    if step:
        aliases = {1 + len(operands) + i: i for i in range(2 * len(roles))}
        for state in states:
            operands += list(state)
    kernel = functools.partial(attend_kernel, roles, step, emit)
    out = call(kernel, "attend_" + "_".join(roles) + str(step), out_shape, mask, operands, aliases)
    return [tuple(out[2 * i : 2 * i + 2]) for i in range(len(roles))], out[2 * len(roles) :]


def fold_kernel(roles, mask_ref, *refs):
    count = len(roles)
    for i, role in enumerate(roles):
        acc_in, top_in, mate_ref = refs[3 * i : 3 * i + 3]
        acc_ref, top_ref = refs[3 * count + 2 * i : 3 * count + 2 * i + 2]
        rows = acc_ref.shape[0]

        def run():
            for h in range(top_ref.shape[1] // HD):
                part, lse = read_message(mate_ref, rows, h * HD)
                acc, top = merge(acc_in[0:rows, wide(h)], top_in[0:rows, tall(h)], part, lse)
                acc_ref[:, wide(h)] = acc
                top_ref[:, tall(h)] = top

        if role == "lent":
            pl.when(lax.axis_index("span") == mask_ref.shape[1] - 2)(run)
        else:
            run()


def fold(mask, roles, states, mates):
    rows, width = mates[0].shape[0] - STAT, mates[0].shape[1]
    operands = [x for state, mate in zip(states, mates) for x in (*state, mate)]
    kernel = functools.partial(fold_kernel, roles)
    out = call(kernel, "fold", state_shape(rows, width) * len(roles), mask, operands)
    return [tuple(out[2 * i : 2 * i + 2]) for i in range(len(roles))]


def last_kernel(role, step, groups, mask_ref, ka_ref, kb_low, kb_high, va_ref, vb_ref, q_ref, acc_in, top_in, *outs):
    rows = q_ref.shape[0]
    visible = visible_of(role, step, mask_ref)

    def store(h, acc, top):
        if role == "own":
            outs[0][:, wide(h)] = acc
            outs[1][:, tall(h)] = top
        else:
            g = 0 if h < groups[1][0] else 1
            write_message(acc, top, outs[g], (h - groups[g][0]) * HD)

    def run(see):
        for h in range(q_ref.shape[1] // HD):
            acc, top = acc_in[:, wide(h)], top_in[:, tall(h)]
            if see:
                low = h < groups[1][0]
                other = kb_low[:, tall(h)] if low else kb_high[:, tall(h - groups[1][0])]
                keys, values = [ka_ref[:, tall(h)], other], [va_ref[:, tall(h)], vb_ref[:, tall(h)]]
                acc, top = update(q_ref[:, tall(h)], keys, values, acc, top)
            store(h, acc, top)

    helps = lax.axis_index("span") == mask_ref.shape[1] - 2
    pl.when(visible)(lambda: run(True))
    pl.when(jnp.logical_not(visible) & (helps if role == "lent" else True))(lambda: run(False))


def attend_last(mask, role, step, groups, keys, values, query, state):
    rows, width = query.shape
    if role == "own":
        out_shape = state_shape(rows, width)
    else:
        out_shape = [message_shape(rows, b - a) for a, b in groups]
    kernel = functools.partial(last_kernel, role, step, groups)
    return call(kernel, "last_" + role, out_shape, mask, [*keys, *values, query, *state])


def join_kernel(part_of_heads, mask_ref, acc_ref, top_ref, msg_ref, out_ref):
    low, high = part_of_heads
    rows = acc_ref.shape[0]

    def run(helped):
        for h in range(low, high):
            acc = acc_ref[:, wide(h)]
            if helped:
                part, lse = read_message(msg_ref, rows, (h - low) * HD)
                acc, _ = merge(acc, top_ref[:, tall(h)], part, lse)
            out_ref[:, tall(h - low)] = (acc[:, :HD] / acc[:, HD:]).astype(jnp.bfloat16)

    helped = lax.axis_index("span") == mask_ref.shape[1] - 1
    pl.when(helped)(lambda: run(True))
    pl.when(jnp.logical_not(helped))(lambda: run(False))


def join(mask, part_of_heads, state, message):
    shape = (state[0].shape[0], (part_of_heads[1] - part_of_heads[0]) * HD)
    kernel = functools.partial(join_kernel, part_of_heads)
    return call(kernel, "join" + str(part_of_heads[0]), [jax.ShapeDtypeStruct(shape, jnp.bfloat16)], mask, [*state, message])[0]


TILE = 512


def project_kernel(lows, step_ref, *refs):
    count = len(lows)
    rows_refs, (w_own, w_mate, w_far, w_back), refs = refs[:count], refs[count : count + 4], refs[count + 4 :]
    straight = lax.axis_index("head") == lax.axis_index("seq")
    last = len(refs) > 1
    if last:
        total_ref, gate_ref, out_ref, stage, sems = refs
        gate_row = pl.ds(step_ref[lax.axis_index("span")], 1)
    else:
        out_ref = refs[0]
    tiles = out_ref.shape[1] // TILE

    def copy(t):
        return pltpu.make_async_copy(stage.at[t], out_ref.at[:, t * TILE : (t + 1) * TILE], sems.at[t])

    def run(w_mine, w_theirs):
        for t in range(tiles):
            lanes = slice(t * TILE, (t + 1) * TILE)
            total = total_ref[:, lanes] if last else None
            for ref, (low, own) in zip(rows_refs, lows):
                weight = w_mine if own else w_theirs
                term = dot(ref[...], weight[low : low + ref.shape[1], lanes], ((1,), (0,)))
                total = term if total is None else total + term
            if last:
                stage[t] = (gate_ref[gate_row, lanes] * total).astype(jnp.bfloat16)
                copy(t).start()
            else:
                out_ref[:, lanes] = total

    pl.when(straight)(lambda: run(w_own, w_back))
    pl.when(jnp.logical_not(straight))(lambda: run(w_mate, w_far))
    if last:
        for t in range(tiles):
            copy(t).wait()


def project(step_index, terms, weights, total=None, gate_table=None):
    rows, columns = terms[0][0].shape[0], weights[0].shape[1]
    last = total is not None
    operands = [x for x, _, _ in terms] + [*weights] + ([total, gate_table] if last else [])
    return pl.pallas_call(
        functools.partial(project_kernel, [(low, own) for _, low, own in terms]),
        out_shape=jax.ShapeDtypeStruct((rows, columns), jnp.bfloat16 if last else jnp.float32),
        in_specs=[pl.BlockSpec(memory_space=pltpu.SMEM)]
        + [pl.BlockSpec(memory_space=pltpu.VMEM)] * len(operands),
        out_specs=pl.BlockSpec(memory_space=pl.ANY if last else pltpu.VMEM),
        scratch_shapes=[
            pltpu.VMEM((columns // TILE, rows, TILE), jnp.bfloat16),
            pltpu.SemaphoreType.DMA((columns // TILE,)),
        ]
        if last
        else [],
        compiler_params=pltpu.CompilerParams(vmem_limit_bytes=VMEM_LIMIT),
        cost_estimate=BRIEF,
        name="project_last" if last else "project_most",
    )(step_index, *operands)


def after(value, done):
    return lax.optimization_barrier((value, done))[0]


def swap_pairs(count):
    return [(i, count - 1 - i) for i in range(count)]


def on_device(query_rows, key_rows, value_rows, out_weight, gate_table, step_index, block_mask):
    heads = query_rows.shape[1] // HD
    spans, cores, sides = lax.axis_size("span"), lax.axis_size("seq"), lax.axis_size("head")
    split = (heads + 1) // 2
    groups = [(0, split), (split, heads)]
    exchange = sides == cores == 2
    final = spans - 2

    def up(x, step):
        return lax.ppermute(x, "span", [(i, i + 1) for i in range(step - 1, spans - 2)])

    def across(x):
        return lax.ppermute(x, "seq", swap_pairs(cores))

    if exchange:
        pair = ("head", "seq")
        w_far = lax.ppermute(out_weight, pair, [(1, 2), (2, 1)])
    asked = lax.ppermute(query_rows, "span", [(spans - 1, spans - 2)])
    query_mate = across(query_rows)
    queries, lent = [query_rows, query_mate], None
    key, value = key_rows, value_rows
    roles = ["lent", "own"]
    for step in range(final):
        key_next, value_next = up(key, step + 1), up(value, step + 1)
        emit = step + 1 == final
        keys = [key_next, *(across(key_next[:, a * HD : b * HD]) for a, b in groups)] if emit else [key_next]
        if step == 0:
            (own,), own_draft = attend(block_mask, ["own"], 0, key, value, queries, [], emit)
            asked = after(asked, (own, key_next, value_next))
            asks = [asked, across(asked)]
            (lent,), lent_draft = attend(block_mask, ["lent"], 0, key, value, asks, [], emit)
            states, drafts = [lent, own], [*lent_draft, *own_draft]
        else:
            waits = [after(asks[0], keys), asks[1], *queries]
            states, drafts = attend(block_mask, roles, step, key, value, waits, states, emit)
        key, value = key_next, value_next
    lent, own = fold(block_mask, roles, states, [across(x) for x in drafts])
    values = [value, across(value)]
    back_up = [(spans - 2, spans - 1)]
    messages = attend_last(block_mask, "lent", final, groups, keys, values, asks[0], lent)
    sent = [lax.ppermute(x, "span", back_up) for x in messages]
    if exchange:
        w_mate = across(after(out_weight, messages[1]))
        w_back = across(after(w_far, messages[1]))
    own = attend_last(block_mask, "own", final, groups, keys, values, after(query_rows, messages), own)
    mine = [join(block_mask, groups[0], own, sent[0])]
    mine.append(join(block_mask, groups[1], own, after(sent[1], mine[0])))

    if exchange:
        theirs = [lax.ppermute(x, "head", swap_pairs(sides)) for x in mine]
        weights, low = [out_weight, w_mate, w_far, w_back], split * HD
        most = [(mine[0], 0, True), (mine[1], low, True), (theirs[0], 0, False)]
        total = project(step_index, most, weights)
        return project(step_index, [(theirs[1], low, False)], weights, total, gate_table)
    weight = lax.all_gather(out_weight, "seq", axis=1, tiled=True)
    projected = jnp.dot(jnp.concatenate(mine, axis=1), weight, preferred_element_type=jnp.float32)
    shared = lax.psum_scatter(projected.astype(jnp.bfloat16), "head", scatter_dimension=1, tiled=True)
    gate_row = gate_table[step_index[lax.axis_index("span")]]
    return (gate_row[None, :] * shared.astype(jnp.float32)).astype(jnp.bfloat16)


def solution(mesh):
    in_specs = (
        P(("streams", "span", "seq"), "head"),
        P(("streams", "span", "seq"), "head"),
        P(("streams", "span", "seq"), "head"),
        P("head", "seq"),
        P(None, "head"),
        P("streams"),
        P("streams", None),
    )
    out_specs = P(("streams", "span", "seq"), "head")
    return jax.shard_map(
        on_device, mesh=mesh, in_specs=in_specs, out_specs=out_specs, check_vma=False
    )
```

```python
import functools
import math

import jax
import jax.numpy as jnp
from jax import lax
from jax.experimental import pallas as pl
from jax.experimental.pallas import tpu as pltpu
from jax.sharding import PartitionSpec as P

HD = 128
NEG = -1e30
STAT = 16
VMEM_LIMIT = 16 * 1024 * 1024
BRIEF = pl.CostEstimate(flops=1, transcendentals=0, bytes_accessed=1)


def dot(a, b, dims):
    return lax.dot_general(a, b, (dims, ((), ())), preferred_element_type=jnp.float32)


def parts_of(x):
    hi = x.astype(jnp.bfloat16)
    rest = x - hi.astype(jnp.float32)
    mid = rest.astype(jnp.bfloat16)
    low = (rest - mid.astype(jnp.float32)).astype(jnp.bfloat16)
    return hi, mid, low


def write_message(acc, top, out_ref, at):
    rows = acc.shape[0]
    lanes = slice(at, at + HD)
    total = acc[:, HD:]
    live = total > 0.0
    safe = jnp.where(live, total, 1.0)
    out_ref[0:rows, lanes] = (acc[:, :HD] / safe).astype(jnp.bfloat16)
    lse = jnp.where(live, top + jnp.log2(safe), NEG)
    hi, mid, low = parts_of(lse)
    lane = lax.broadcasted_iota(jnp.int32, lse.shape, 1)
    zero = jnp.zeros_like(hi)
    packed = jnp.where(lane == 0, hi, jnp.where(lane == 1, mid, jnp.where(lane == 2, low, zero)))
    row = lax.broadcasted_iota(jnp.int32, (STAT, HD), 0)
    col = lax.broadcasted_iota(jnp.int32, (STAT, HD), 1)
    stats = jnp.zeros((STAT, HD), jnp.float32)
    for block in range(rows // HD):
        pick = jnp.where((row - 3 * block == col) & (col < 3), 1.0, 0.0).astype(jnp.bfloat16)
        stats += dot(pick, packed[block * HD : (block + 1) * HD], ((1,), (1,)))
    out_ref[rows:, lanes] = stats.astype(jnp.bfloat16)


def read_message(msg_ref, rows, at):
    lanes = slice(at, at + HD)
    row = lax.broadcasted_iota(jnp.int32, (STAT, HD), 0)
    blocks = []
    for block in range(rows // HD):
        pick = jnp.where((row >= 3 * block) & (row < 3 * block + 3), 1.0, 0.0).astype(jnp.bfloat16)
        blocks.append(dot(msg_ref[rows:, lanes], pick, ((0,), (0,))))
    return msg_ref[0:rows, lanes].astype(jnp.float32), jnp.concatenate(blocks, axis=0)


def visible_of(role, step, mask_ref):
    span, spans = lax.axis_index("span"), mask_ref.shape[1]
    keys = jnp.maximum(span - step, 0)
    if role == "own":
        there = (span >= step) if step == 0 else (span >= step) & (span != spans - 1)
        return there & (mask_ref[span, keys] == 1)
    return (span == spans - 2) & (span >= step) & (mask_ref[spans - 1, keys] == 1)


def wide(h):
    return slice(2 * h * HD, 2 * (h + 1) * HD)


def update(q, keys, values, acc, top):
    scale = math.log2(math.e) / math.sqrt(HD)
    scores = [dot(q, k, ((1,), (1,))) for k in keys]
    peak = functools.reduce(jnp.maximum, scores) if len(scores) > 1 else scores[0]
    peak = jnp.broadcast_to(jnp.max(peak, axis=1, keepdims=True) * scale, (q.shape[0], HD))
    new_top = peak if top is None else jnp.maximum(top, peak)
    total = None
    for score, v in zip(scores, values):
        line = jnp.concatenate([new_top] * (v.shape[0] // HD), axis=1)
        prob = jnp.exp2(score * scale - line).astype(jnp.bfloat16)
        wide_v = jnp.concatenate([v, jnp.ones(v.shape, jnp.bfloat16)], axis=1)
        term = dot(prob, wide_v, ((1,), (0,)))
        total = term if total is None else total + term
    if top is not None:
        fade = jnp.exp2(top - new_top)
        total += acc * jnp.concatenate([fade, fade], axis=1)
    return total, new_top


def merge(acc, top, part, lse):
    peak = jnp.maximum(top, lse)
    mine = jnp.exp2(top - peak)
    theirs = jnp.where(lse > 0.5 * NEG, jnp.exp2(lse - peak), 0.0)
    return (
        acc * jnp.concatenate([mine, mine], axis=1) + jnp.concatenate([part * theirs, theirs], axis=1),
        peak,
    )


def tall(h):
    return slice(h * HD, (h + 1) * HD)


def attend_kernel(roles, step, emit, mask_ref, k_ref, v_ref, *refs):
    q_refs, refs = refs[: 2 * len(roles)], refs[2 * len(roles) :]
    if step:
        refs = refs[2 * len(roles) :]
    drafts = refs[2 * len(roles) :]
    rows, heads = q_refs[0].shape[0], k_ref.shape[1] // HD
    for i, role in enumerate(roles):
        acc_ref, top_ref = refs[2 * i : 2 * i + 2]
        visible = visible_of(role, step, mask_ref)

        @pl.when(visible)
        def _():
            for h in range(heads):
                for half in range(2):
                    at = slice(half * rows, (half + 1) * rows)
                    acc, top = (acc_ref[at, wide(h)], top_ref[at, tall(h)]) if step else (None, None)
                    acc, top = update(q_refs[2 * i + half][:, tall(h)], [k_ref[:, tall(h)]], [v_ref[:, tall(h)]], acc, top)
                    acc_ref[at, wide(h)] = acc
                    top_ref[at, tall(h)] = top

        if step == 0:

            @pl.when(jnp.logical_not(visible))
            def _():
                acc_ref[...] = jnp.zeros(acc_ref.shape, jnp.float32)
                top_ref[...] = jnp.full(top_ref.shape, NEG, jnp.float32)

        if emit:
            def write():
                for h in range(heads):
                    write_message(acc_ref[rows:, wide(h)], top_ref[rows:, tall(h)], drafts[i], h * HD)

            if role == "lent":
                pl.when(lax.axis_index("span") == mask_ref.shape[1] - 2)(write)
            else:
                write()


def call(kernel, name, out_shape, mask, operands, aliases=None):
    return pl.pallas_call(
        kernel,
        out_shape=out_shape,
        in_specs=[pl.BlockSpec(memory_space=pltpu.SMEM)] + [pl.BlockSpec(memory_space=pltpu.VMEM)] * len(operands),
        out_specs=[pl.BlockSpec(memory_space=pltpu.VMEM)] * len(out_shape),
        input_output_aliases=aliases or {},
        compiler_params=pltpu.CompilerParams(vmem_limit_bytes=VMEM_LIMIT),
        cost_estimate=BRIEF,
        name=name,
    )(mask, *operands)


def state_shape(rows, width):
    return [
        jax.ShapeDtypeStruct((rows, 2 * width), jnp.float32),
        jax.ShapeDtypeStruct((rows, width), jnp.float32),
    ]


def message_shape(rows, heads):
    return jax.ShapeDtypeStruct((rows + STAT, heads * HD), jnp.bfloat16)


def attend(mask, roles, step, key, value, queries, states, emit):
    rows, width = key.shape
    out_shape = state_shape(2 * rows, width) * len(roles)
    if emit:
        out_shape = out_shape + [message_shape(rows, width // HD)] * len(roles)
    operands = [key, value, *queries]
    aliases = {}
    if step:
        aliases = {1 + len(operands) + i: i for i in range(2 * len(roles))}
        for state in states:
            operands += list(state)
    kernel = functools.partial(attend_kernel, roles, step, emit)
    out = call(kernel, "attend_" + "_".join(roles) + str(step), out_shape, mask, operands, aliases)
    return [tuple(out[2 * i : 2 * i + 2]) for i in range(len(roles))], out[2 * len(roles) :]


def fold_kernel(roles, mask_ref, *refs):
    count = len(roles)
    for i, role in enumerate(roles):
        acc_in, top_in, mate_ref = refs[3 * i : 3 * i + 3]
        acc_ref, top_ref = refs[3 * count + 2 * i : 3 * count + 2 * i + 2]
        rows = acc_ref.shape[0]

        def run():
            for h in range(top_ref.shape[1] // HD):
                part, lse = read_message(mate_ref, rows, h * HD)
                acc, top = merge(acc_in[0:rows, wide(h)], top_in[0:rows, tall(h)], part, lse)
                acc_ref[:, wide(h)] = acc
                top_ref[:, tall(h)] = top

        if role == "lent":
            pl.when(lax.axis_index("span") == mask_ref.shape[1] - 2)(run)
        else:
            run()


def fold(mask, roles, states, mates):
    rows, width = mates[0].shape[0] - STAT, mates[0].shape[1]
    operands = [x for state, mate in zip(states, mates) for x in (*state, mate)]
    kernel = functools.partial(fold_kernel, roles)
    out = call(kernel, "fold", state_shape(rows, width) * len(roles), mask, operands)
    return [tuple(out[2 * i : 2 * i + 2]) for i in range(len(roles))]


def last_kernel(role, step, groups, mask_ref, ka_ref, kb_low, kb_high, va_ref, vb_ref, q_ref, acc_in, top_in, *outs):
    rows = q_ref.shape[0]
    visible = visible_of(role, step, mask_ref)

    def store(h, acc, top):
        if role == "own":
            outs[0][:, wide(h)] = acc
            outs[1][:, tall(h)] = top
        else:
            g = 0 if h < groups[1][0] else 1
            write_message(acc, top, outs[g], (h - groups[g][0]) * HD)

    def run(see):
        for h in range(q_ref.shape[1] // HD):
            acc, top = acc_in[:, wide(h)], top_in[:, tall(h)]
            if see:
                low = h < groups[1][0]
                other = kb_low[:, tall(h)] if low else kb_high[:, tall(h - groups[1][0])]
                keys, values = [ka_ref[:, tall(h)], other], [va_ref[:, tall(h)], vb_ref[:, tall(h)]]
                acc, top = update(q_ref[:, tall(h)], keys, values, acc, top)
            store(h, acc, top)

    helps = lax.axis_index("span") == mask_ref.shape[1] - 2
    pl.when(visible)(lambda: run(True))
    pl.when(jnp.logical_not(visible) & (helps if role == "lent" else True))(lambda: run(False))


def attend_last(mask, role, step, groups, keys, values, query, state):
    rows, width = query.shape
    if role == "own":
        out_shape = state_shape(rows, width)
    else:
        out_shape = [message_shape(rows, b - a) for a, b in groups]
    kernel = functools.partial(last_kernel, role, step, groups)
    return call(kernel, "last_" + role, out_shape, mask, [*keys, *values, query, *state])


def join_kernel(part_of_heads, mask_ref, acc_ref, top_ref, msg_ref, out_ref):
    low, high = part_of_heads
    rows = acc_ref.shape[0]

    def run(helped):
        for h in range(low, high):
            acc = acc_ref[:, wide(h)]
            if helped:
                part, lse = read_message(msg_ref, rows, (h - low) * HD)
                acc, _ = merge(acc, top_ref[:, tall(h)], part, lse)
            out_ref[:, tall(h - low)] = (acc[:, :HD] / acc[:, HD:]).astype(jnp.bfloat16)

    helped = lax.axis_index("span") == mask_ref.shape[1] - 1
    pl.when(helped)(lambda: run(True))
    pl.when(jnp.logical_not(helped))(lambda: run(False))


def join(mask, part_of_heads, state, message):
    shape = (state[0].shape[0], (part_of_heads[1] - part_of_heads[0]) * HD)
    kernel = functools.partial(join_kernel, part_of_heads)
    return call(kernel, "join" + str(part_of_heads[0]), [jax.ShapeDtypeStruct(shape, jnp.bfloat16)], mask, [*state, message])[0]


TILE = 512


def project_kernel(lows, step_ref, *refs):
    count = len(lows)
    rows_refs, (w_own, w_mate, w_far, w_back), refs = refs[:count], refs[count : count + 4], refs[count + 4 :]
    straight = lax.axis_index("head") == lax.axis_index("seq")
    last, added = len(refs) > 2, len(refs) > 1
    total_ref = refs[0] if added else None
    if last:
        total_ref, gate_ref, out_ref, stage, sems = refs
        gate_row = pl.ds(step_ref[lax.axis_index("span")], 1)
    else:
        out_ref = refs[-1]
    tiles = out_ref.shape[1] // TILE

    def copy(t):
        return pltpu.make_async_copy(stage.at[t], out_ref.at[:, t * TILE : (t + 1) * TILE], sems.at[t])

    def run(w_mine, w_theirs):
        for t in range(tiles):
            lanes = slice(t * TILE, (t + 1) * TILE)
            total = total_ref[:, lanes] if added else None
            for ref, (low, own) in zip(rows_refs, lows):
                weight = w_mine if own else w_theirs
                term = dot(ref[...], weight[low : low + ref.shape[1], lanes], ((1,), (0,)))
                total = term if total is None else total + term
            if last:
                stage[t] = (gate_ref[gate_row, lanes] * total).astype(jnp.bfloat16)
                copy(t).start()
            else:
                out_ref[:, lanes] = total

    pl.when(straight)(lambda: run(w_own, w_back))
    pl.when(jnp.logical_not(straight))(lambda: run(w_mate, w_far))
    if last:
        for t in range(tiles):
            copy(t).wait()


def project(step_index, terms, weights, total=None, gate_table=None):
    rows, columns = terms[0][0].shape[0], weights[0].shape[1]
    last = gate_table is not None
    operands = [x for x, _, _ in terms] + [*weights] + [x for x in (total, gate_table) if x is not None]
    return pl.pallas_call(
        functools.partial(project_kernel, [(low, own) for _, low, own in terms]),
        out_shape=jax.ShapeDtypeStruct((rows, columns), jnp.bfloat16 if last else jnp.float32),
        in_specs=[pl.BlockSpec(memory_space=pltpu.SMEM)]
        + [pl.BlockSpec(memory_space=pltpu.VMEM)] * len(operands),
        out_specs=pl.BlockSpec(memory_space=pl.ANY if last else pltpu.VMEM),
        scratch_shapes=[
            pltpu.VMEM((columns // TILE, rows, TILE), jnp.bfloat16),
            pltpu.SemaphoreType.DMA((columns // TILE,)),
        ]
        if last
        else [],
        compiler_params=pltpu.CompilerParams(vmem_limit_bytes=VMEM_LIMIT),
        cost_estimate=BRIEF,
        name="project_last" if last else "project_most" if total is None else "project_more",
    )(step_index, *operands)


def after(value, done):
    return lax.optimization_barrier((value, done))[0]


def swap_pairs(count):
    return [(i, count - 1 - i) for i in range(count)]


def on_device(query_rows, key_rows, value_rows, out_weight, gate_table, step_index, block_mask):
    heads = query_rows.shape[1] // HD
    spans, cores, sides = lax.axis_size("span"), lax.axis_size("seq"), lax.axis_size("head")
    split = (heads + 1) // 2
    groups = [(0, split), (split, heads)]
    exchange = sides == cores == 2
    final = spans - 2

    def up(x, step):
        return lax.ppermute(x, "span", [(i, i + 1) for i in range(step - 1, spans - 2)])

    def across(x):
        return lax.ppermute(x, "seq", swap_pairs(cores))

    if exchange:
        pair = ("head", "seq")
        w_far = lax.ppermute(out_weight, pair, [(1, 2), (2, 1)])
    asked = lax.ppermute(query_rows, "span", [(spans - 1, spans - 2)])
    query_mate = across(query_rows)
    queries, lent = [query_rows, query_mate], None
    key, value = key_rows, value_rows
    roles = ["lent", "own"]
    for step in range(final):
        key_next, value_next = up(key, step + 1), up(value, step + 1)
        emit = step + 1 == final
        keys = [key_next, *(across(key_next[:, a * HD : b * HD]) for a, b in groups)] if emit else [key_next]
        if step == 0:
            (own,), own_draft = attend(block_mask, ["own"], 0, key, value, queries, [], emit)
            asked = after(asked, (own, key_next, value_next))
            asks = [asked, across(asked)]
            (lent,), lent_draft = attend(block_mask, ["lent"], 0, key, value, asks, [], emit)
            states, drafts = [lent, own], [*lent_draft, *own_draft]
        else:
            waits = [after(asks[0], keys), asks[1], *queries]
            states, drafts = attend(block_mask, roles, step, key, value, waits, states, emit)
        key, value = key_next, value_next
    lent, own = fold(block_mask, roles, states, [across(x) for x in drafts])
    values = [value, across(value)]
    back_up = [(spans - 2, spans - 1)]
    messages = attend_last(block_mask, "lent", final, groups, keys, values, asks[0], lent)
    sent = [lax.ppermute(x, "span", back_up) for x in messages]
    if exchange:
        w_mate = across(after(out_weight, messages[1]))
        w_back = across(after(w_far, messages[1]))
    own = attend_last(block_mask, "own", final, groups, keys, values, after(query_rows, messages), own)
    mine = [join(block_mask, groups[0], own, sent[0])]
    mine.append(join(block_mask, groups[1], own, after(sent[1], mine[0])))

    if exchange:
        theirs = [lax.ppermute(x, "head", swap_pairs(sides)) for x in mine]
        weights, low = [out_weight, w_mate, w_far, w_back], split * HD
        total = project(step_index, [(mine[0], 0, True), (mine[1], low, True)], weights)
        total = project(step_index, [(theirs[0], 0, False)], weights, total)
        return project(step_index, [(theirs[1], low, False)], weights, total, gate_table)
    weight = lax.all_gather(out_weight, "seq", axis=1, tiled=True)
    projected = jnp.dot(jnp.concatenate(mine, axis=1), weight, preferred_element_type=jnp.float32)
    shared = lax.psum_scatter(projected.astype(jnp.bfloat16), "head", scatter_dimension=1, tiled=True)
    gate_row = gate_table[step_index[lax.axis_index("span")]]
    return (gate_row[None, :] * shared.astype(jnp.float32)).astype(jnp.bfloat16)


def solution(mesh):
    in_specs = (
        P(("streams", "span", "seq"), "head"),
        P(("streams", "span", "seq"), "head"),
        P(("streams", "span", "seq"), "head"),
        P("head", "seq"),
        P(None, "head"),
        P("streams"),
        P("streams", None),
    )
    out_specs = P(("streams", "span", "seq"), "head")
    return jax.shard_map(
        on_device, mesh=mesh, in_specs=in_specs, out_specs=out_specs, check_vma=False
    )
```

```python
import functools
import math

import jax
import jax.numpy as jnp
from jax import lax
from jax.experimental import pallas as pl
from jax.experimental.pallas import tpu as pltpu
from jax.sharding import PartitionSpec as P

HD = 128
NEG = -1e30
STAT = 16
VMEM_LIMIT = 16 * 1024 * 1024
BRIEF = pl.CostEstimate(flops=1, transcendentals=0, bytes_accessed=1)


def dot(a, b, dims):
    return lax.dot_general(a, b, (dims, ((), ())), preferred_element_type=jnp.float32)


def parts_of(x):
    hi = x.astype(jnp.bfloat16)
    rest = x - hi.astype(jnp.float32)
    mid = rest.astype(jnp.bfloat16)
    low = (rest - mid.astype(jnp.float32)).astype(jnp.bfloat16)
    return hi, mid, low


def write_message(acc, top, out_ref, at):
    rows = acc.shape[0]
    lanes = slice(at, at + HD)
    total = acc[:, HD:]
    live = total > 0.0
    safe = jnp.where(live, total, 1.0)
    out_ref[0:rows, lanes] = (acc[:, :HD] / safe).astype(jnp.bfloat16)
    lse = jnp.where(live, top + jnp.log2(safe), NEG)
    hi, mid, low = parts_of(lse)
    lane = lax.broadcasted_iota(jnp.int32, lse.shape, 1)
    zero = jnp.zeros_like(hi)
    packed = jnp.where(lane == 0, hi, jnp.where(lane == 1, mid, jnp.where(lane == 2, low, zero)))
    row = lax.broadcasted_iota(jnp.int32, (STAT, HD), 0)
    col = lax.broadcasted_iota(jnp.int32, (STAT, HD), 1)
    stats = jnp.zeros((STAT, HD), jnp.float32)
    for block in range(rows // HD):
        pick = jnp.where((row - 3 * block == col) & (col < 3), 1.0, 0.0).astype(jnp.bfloat16)
        stats += dot(pick, packed[block * HD : (block + 1) * HD], ((1,), (1,)))
    out_ref[rows:, lanes] = stats.astype(jnp.bfloat16)


def read_message(msg_ref, rows, at):
    lanes = slice(at, at + HD)
    row = lax.broadcasted_iota(jnp.int32, (STAT, HD), 0)
    blocks = []
    for block in range(rows // HD):
        pick = jnp.where((row >= 3 * block) & (row < 3 * block + 3), 1.0, 0.0).astype(jnp.bfloat16)
        blocks.append(dot(msg_ref[rows:, lanes], pick, ((0,), (0,))))
    return msg_ref[0:rows, lanes].astype(jnp.float32), jnp.concatenate(blocks, axis=0)


def visible_of(role, step, mask_ref):
    span, spans = lax.axis_index("span"), mask_ref.shape[1]
    keys = jnp.maximum(span - step, 0)
    if role == "own":
        there = (span >= step) if step == 0 else (span >= step) & (span != spans - 1)
        return there & (mask_ref[span, keys] == 1)
    return (span == spans - 2) & (span >= step) & (mask_ref[spans - 1, keys] == 1)


def wide(h):
    return slice(2 * h * HD, 2 * (h + 1) * HD)


def update(q, keys, values, acc, top):
    scale = math.log2(math.e) / math.sqrt(HD)
    scores = [dot(q, k, ((1,), (1,))) for k in keys]
    peak = functools.reduce(jnp.maximum, scores) if len(scores) > 1 else scores[0]
    peak = jnp.broadcast_to(jnp.max(peak, axis=1, keepdims=True) * scale, (q.shape[0], HD))
    new_top = peak if top is None else jnp.maximum(top, peak)
    total = None
    for score, v in zip(scores, values):
        line = jnp.concatenate([new_top] * (v.shape[0] // HD), axis=1)
        prob = jnp.exp2(score * scale - line).astype(jnp.bfloat16)
        wide_v = jnp.concatenate([v, jnp.ones(v.shape, jnp.bfloat16)], axis=1)
        term = dot(prob, wide_v, ((1,), (0,)))
        total = term if total is None else total + term
    if top is not None:
        fade = jnp.exp2(top - new_top)
        total += acc * jnp.concatenate([fade, fade], axis=1)
    return total, new_top


def merge(acc, top, part, lse):
    peak = jnp.maximum(top, lse)
    mine = jnp.exp2(top - peak)
    theirs = jnp.where(lse > 0.5 * NEG, jnp.exp2(lse - peak), 0.0)
    return (
        acc * jnp.concatenate([mine, mine], axis=1) + jnp.concatenate([part * theirs, theirs], axis=1),
        peak,
    )


def tall(h):
    return slice(h * HD, (h + 1) * HD)


def attend_kernel(roles, step, emit, mask_ref, k_ref, v_ref, *refs):
    q_refs, refs = refs[: 2 * len(roles)], refs[2 * len(roles) :]
    if step:
        refs = refs[2 * len(roles) :]
    drafts = refs[2 * len(roles) :]
    rows, heads = q_refs[0].shape[0], k_ref.shape[1] // HD
    for i, role in enumerate(roles):
        acc_ref, top_ref = refs[2 * i : 2 * i + 2]
        visible = visible_of(role, step, mask_ref)

        @pl.when(visible)
        def _():
            for h in range(heads):
                for half in range(2):
                    at = slice(half * rows, (half + 1) * rows)
                    acc, top = (acc_ref[at, wide(h)], top_ref[at, tall(h)]) if step else (None, None)
                    acc, top = update(q_refs[2 * i + half][:, tall(h)], [k_ref[:, tall(h)]], [v_ref[:, tall(h)]], acc, top)
                    acc_ref[at, wide(h)] = acc
                    top_ref[at, tall(h)] = top

        if step == 0:

            @pl.when(jnp.logical_not(visible))
            def _():
                acc_ref[...] = jnp.zeros(acc_ref.shape, jnp.float32)
                top_ref[...] = jnp.full(top_ref.shape, NEG, jnp.float32)

        if emit:
            def write():
                for h in range(heads):
                    write_message(acc_ref[rows:, wide(h)], top_ref[rows:, tall(h)], drafts[i], h * HD)

            if role == "lent":
                pl.when(lax.axis_index("span") == mask_ref.shape[1] - 2)(write)
            else:
                write()


def call(kernel, name, out_shape, mask, operands, aliases=None):
    return pl.pallas_call(
        kernel,
        out_shape=out_shape,
        in_specs=[pl.BlockSpec(memory_space=pltpu.SMEM)] + [pl.BlockSpec(memory_space=pltpu.VMEM)] * len(operands),
        out_specs=[pl.BlockSpec(memory_space=pltpu.VMEM)] * len(out_shape),
        input_output_aliases=aliases or {},
        compiler_params=pltpu.CompilerParams(vmem_limit_bytes=VMEM_LIMIT),
        cost_estimate=BRIEF,
        name=name,
    )(mask, *operands)


def state_shape(rows, width):
    return [
        jax.ShapeDtypeStruct((rows, 2 * width), jnp.float32),
        jax.ShapeDtypeStruct((rows, width), jnp.float32),
    ]


def message_shape(rows, heads):
    return jax.ShapeDtypeStruct((rows + STAT, heads * HD), jnp.bfloat16)


def attend(mask, roles, step, key, value, queries, states, emit):
    rows, width = key.shape
    out_shape = state_shape(2 * rows, width) * len(roles)
    if emit:
        out_shape = out_shape + [message_shape(rows, width // HD)] * len(roles)
    operands = [key, value, *queries]
    aliases = {}
    if step:
        aliases = {1 + len(operands) + i: i for i in range(2 * len(roles))}
        for state in states:
            operands += list(state)
    kernel = functools.partial(attend_kernel, roles, step, emit)
    out = call(kernel, "attend_" + "_".join(roles) + str(step), out_shape, mask, operands, aliases)
    return [tuple(out[2 * i : 2 * i + 2]) for i in range(len(roles))], out[2 * len(roles) :]


def fold_kernel(roles, mask_ref, *refs):
    count = len(roles)
    for i, role in enumerate(roles):
        acc_in, top_in, mate_ref = refs[3 * i : 3 * i + 3]
        acc_ref, top_ref = refs[3 * count + 2 * i : 3 * count + 2 * i + 2]
        rows = acc_ref.shape[0]

        def run():
            for h in range(top_ref.shape[1] // HD):
                part, lse = read_message(mate_ref, rows, h * HD)
                acc, top = merge(acc_in[0:rows, wide(h)], top_in[0:rows, tall(h)], part, lse)
                acc_ref[:, wide(h)] = acc
                top_ref[:, tall(h)] = top

        if role == "lent":
            pl.when(lax.axis_index("span") == mask_ref.shape[1] - 2)(run)
        else:
            run()


def fold(mask, roles, states, mates):
    rows, width = mates[0].shape[0] - STAT, mates[0].shape[1]
    operands = [x for state, mate in zip(states, mates) for x in (*state, mate)]
    kernel = functools.partial(fold_kernel, roles)
    out = call(kernel, "fold", state_shape(rows, width) * len(roles), mask, operands)
    return [tuple(out[2 * i : 2 * i + 2]) for i in range(len(roles))]


def last_kernel(role, step, groups, mask_ref, ka_ref, kb_low, kb_high, va_ref, vb_ref, q_ref, acc_in, top_in, *outs):
    rows = q_ref.shape[0]
    visible = visible_of(role, step, mask_ref)

    def store(h, acc, top):
        if role == "own":
            outs[0][:, wide(h)] = acc
            outs[1][:, tall(h)] = top
        else:
            g = 0 if h < groups[1][0] else 1
            write_message(acc, top, outs[g], (h - groups[g][0]) * HD)

    def run(see):
        for h in range(q_ref.shape[1] // HD):
            acc, top = acc_in[:, wide(h)], top_in[:, tall(h)]
            if see:
                low = h < groups[1][0]
                other = kb_low[:, tall(h)] if low else kb_high[:, tall(h - groups[1][0])]
                keys, values = [ka_ref[:, tall(h)], other], [va_ref[:, tall(h)], vb_ref[:, tall(h)]]
                acc, top = update(q_ref[:, tall(h)], keys, values, acc, top)
            store(h, acc, top)

    helps = lax.axis_index("span") == mask_ref.shape[1] - 2
    pl.when(visible)(lambda: run(True))
    pl.when(jnp.logical_not(visible) & (helps if role == "lent" else True))(lambda: run(False))


def attend_last(mask, role, step, groups, keys, values, query, state):
    rows, width = query.shape
    if role == "own":
        out_shape = state_shape(rows, width)
    else:
        out_shape = [message_shape(rows, b - a) for a, b in groups]
    kernel = functools.partial(last_kernel, role, step, groups)
    return call(kernel, "last_" + role, out_shape, mask, [*keys, *values, query, *state])


def join_kernel(part_of_heads, mask_ref, acc_ref, top_ref, msg_ref, out_ref):
    low, high = part_of_heads
    rows = acc_ref.shape[0]

    def run(helped):
        for h in range(low, high):
            acc = acc_ref[:, wide(h)]
            if helped:
                part, lse = read_message(msg_ref, rows, (h - low) * HD)
                acc, _ = merge(acc, top_ref[:, tall(h)], part, lse)
            out_ref[:, tall(h - low)] = (acc[:, :HD] / acc[:, HD:]).astype(jnp.bfloat16)

    helped = lax.axis_index("span") == mask_ref.shape[1] - 1
    pl.when(helped)(lambda: run(True))
    pl.when(jnp.logical_not(helped))(lambda: run(False))


def join(mask, part_of_heads, state, message):
    shape = (state[0].shape[0], (part_of_heads[1] - part_of_heads[0]) * HD)
    kernel = functools.partial(join_kernel, part_of_heads)
    return call(kernel, "join" + str(part_of_heads[0]), [jax.ShapeDtypeStruct(shape, jnp.bfloat16)], mask, [*state, message])[0]


TILE = 256


def project_kernel(lows, step_ref, *refs):
    count = len(lows)
    rows_refs, (w_own, w_mate, w_far, w_back), refs = refs[:count], refs[count : count + 4], refs[count + 4 :]
    straight = lax.axis_index("head") == lax.axis_index("seq")
    last, added = len(refs) > 2, len(refs) > 1
    total_ref = refs[0] if added else None
    if last:
        total_ref, gate_ref, out_ref, stage, sems = refs
        gate_row = pl.ds(step_ref[lax.axis_index("span")], 1)
    else:
        out_ref = refs[-1]
    tiles = out_ref.shape[1] // TILE

    def copy(t):
        return pltpu.make_async_copy(stage.at[t], out_ref.at[:, t * TILE : (t + 1) * TILE], sems.at[t])

    def run(w_mine, w_theirs):
        for t in range(tiles):
            lanes = slice(t * TILE, (t + 1) * TILE)
            total = total_ref[:, lanes] if added else None
            for ref, (low, own) in zip(rows_refs, lows):
                weight = w_mine if own else w_theirs
                term = dot(ref[...], weight[low : low + ref.shape[1], lanes], ((1,), (0,)))
                total = term if total is None else total + term
            if last:
                stage[t] = (gate_ref[gate_row, lanes] * total).astype(jnp.bfloat16)
                copy(t).start()
            else:
                out_ref[:, lanes] = total

    pl.when(straight)(lambda: run(w_own, w_back))
    pl.when(jnp.logical_not(straight))(lambda: run(w_mate, w_far))
    if last:
        for t in range(tiles):
            copy(t).wait()


def project(step_index, terms, weights, total=None, gate_table=None):
    rows, columns = terms[0][0].shape[0], weights[0].shape[1]
    last = gate_table is not None
    operands = [x for x, _, _ in terms] + [*weights] + [x for x in (total, gate_table) if x is not None]
    return pl.pallas_call(
        functools.partial(project_kernel, [(low, own) for _, low, own in terms]),
        out_shape=jax.ShapeDtypeStruct((rows, columns), jnp.bfloat16 if last else jnp.float32),
        in_specs=[pl.BlockSpec(memory_space=pltpu.SMEM)]
        + [pl.BlockSpec(memory_space=pltpu.VMEM)] * len(operands),
        out_specs=pl.BlockSpec(memory_space=pl.ANY if last else pltpu.VMEM),
        scratch_shapes=[
            pltpu.VMEM((columns // TILE, rows, TILE), jnp.bfloat16),
            pltpu.SemaphoreType.DMA((columns // TILE,)),
        ]
        if last
        else [],
        compiler_params=pltpu.CompilerParams(vmem_limit_bytes=VMEM_LIMIT),
        cost_estimate=BRIEF,
        name="project_last" if last else "project_most" if total is None else "project_more",
    )(step_index, *operands)


def after(value, done):
    return lax.optimization_barrier((value, done))[0]


def swap_pairs(count):
    return [(i, count - 1 - i) for i in range(count)]


def on_device(query_rows, key_rows, value_rows, out_weight, gate_table, step_index, block_mask):
    heads = query_rows.shape[1] // HD
    spans, cores, sides = lax.axis_size("span"), lax.axis_size("seq"), lax.axis_size("head")
    split = (heads + 1) // 2
    groups = [(0, split), (split, heads)]
    exchange = sides == cores == 2
    final = spans - 2

    def up(x, step):
        return lax.ppermute(x, "span", [(i, i + 1) for i in range(step - 1, spans - 2)])

    def across(x):
        return lax.ppermute(x, "seq", swap_pairs(cores))

    if exchange:
        pair = ("head", "seq")
        w_far = lax.ppermute(out_weight, pair, [(1, 2), (2, 1)])
    asked = lax.ppermute(query_rows, "span", [(spans - 1, spans - 2)])
    query_mate = across(query_rows)
    queries, lent = [query_rows, query_mate], None
    key, value = key_rows, value_rows
    roles = ["lent", "own"]
    for step in range(final):
        key_next, value_next = up(key, step + 1), up(value, step + 1)
        emit = step + 1 == final
        keys = [key_next, *(across(key_next[:, a * HD : b * HD]) for a, b in groups)] if emit else [key_next]
        if step == 0:
            (own,), own_draft = attend(block_mask, ["own"], 0, key, value, queries, [], emit)
            asked = after(asked, (own, key_next, value_next))
            asks = [asked, across(asked)]
            (lent,), lent_draft = attend(block_mask, ["lent"], 0, key, value, asks, [], emit)
            states, drafts = [lent, own], [*lent_draft, *own_draft]
        else:
            waits = [after(asks[0], keys), asks[1], *queries]
            states, drafts = attend(block_mask, roles, step, key, value, waits, states, emit)
        key, value = key_next, value_next
    lent, own = fold(block_mask, roles, states, [across(x) for x in drafts])
    values = [value, across(value)]
    back_up = [(spans - 2, spans - 1)]
    messages = attend_last(block_mask, "lent", final, groups, keys, values, asks[0], lent)
    sent = [lax.ppermute(x, "span", back_up) for x in messages]
    if exchange:
        w_mate = across(after(out_weight, messages[1]))
        w_back = across(after(w_far, messages[1]))
    own = attend_last(block_mask, "own", final, groups, keys, values, after(query_rows, messages), own)
    mine = [join(block_mask, groups[0], own, sent[0])]
    mine.append(join(block_mask, groups[1], own, after(sent[1], mine[0])))

    if exchange:
        theirs = [lax.ppermute(x, "head", swap_pairs(sides)) for x in mine]
        weights, low = [out_weight, w_mate, w_far, w_back], split * HD
        total = project(step_index, [(mine[0], 0, True), (mine[1], low, True)], weights)
        total = project(step_index, [(theirs[0], 0, False)], weights, total)
        return project(step_index, [(theirs[1], low, False)], weights, total, gate_table)
    weight = lax.all_gather(out_weight, "seq", axis=1, tiled=True)
    projected = jnp.dot(jnp.concatenate(mine, axis=1), weight, preferred_element_type=jnp.float32)
    shared = lax.psum_scatter(projected.astype(jnp.bfloat16), "head", scatter_dimension=1, tiled=True)
    gate_row = gate_table[step_index[lax.axis_index("span")]]
    return (gate_row[None, :] * shared.astype(jnp.float32)).astype(jnp.bfloat16)


def solution(mesh):
    in_specs = (
        P(("streams", "span", "seq"), "head"),
        P(("streams", "span", "seq"), "head"),
        P(("streams", "span", "seq"), "head"),
        P("head", "seq"),
        P(None, "head"),
        P("streams"),
        P("streams", None),
    )
    out_specs = P(("streams", "span", "seq"), "head")
    return jax.shard_map(
        on_device, mesh=mesh, in_specs=in_specs, out_specs=out_specs, check_vma=False
    )
```
